32 devices in a mesh: row: 4 (over y, x), col: 8 (over z, core).
Axes of the slice: x: 2, y: 2, z: 4, core: 2. Of those that a mesh axis runs over, the one named last changes fastest.
Arguments:
- left_panel: float32 [4096, 8192], P('col', 'row'), may hold values from -6 to 6
- right_panel: float32 [4096, 16384], P('row', 'col'), may hold values from -0.09375 to 0.09375
- arc_basis: float32 [4096, 256], replicated, as said below
- normal_block: float32 [8192, 16384], P('row', 'col'), may hold values from -6 to 6
Outputs:
- updated_block: float32 [8192, 16384], P('row', 'col')
- left_reduced: float32 [4096, 8192], P('col', 'row')
- right_reduced: float32 [4096, 16384], P('row', 'col')
The draws below stay inside these ranges and needn't reach their ends.
Inputs may be any that keep to these rules, and one draw needn't show every extreme that they name: arc_basis has orthonormal columns: arc_basis^T arc_basis equals the 256 x 256 identity within float32 rounding.
All inputs are finite; a program needn't handle non-finite values.
Results may differ from the reference program's by a relative error of at most 0.00005.
Values sent between devices are 32-bit elements; how exact they have to be, the bound alone decides.
A program may use at most 192 MiB of HBM per device.

```python
import jax
import jax.numpy as jnp
from jax import lax

M = 4096
NL = 8192
NR = 16384
K = 256


def cholesky_pass(columns):
    gram = jnp.dot(columns.T, columns, precision=lax.Precision.HIGHEST, preferred_element_type=jnp.float32)
    factor = jnp.linalg.cholesky(gram)
    solved = jax.scipy.linalg.solve_triangular(factor, columns.T, lower=True)
    return solved.T


def draw_arc_basis(key, part):
    first = jax.random.fold_in(jax.random.fold_in(key, 7301), 0)
    raw = jax.random.normal(first, (M, K), jnp.float32)
    raw = raw * M ** (-0.5)
    return cholesky_pass(cholesky_pass(raw)).astype(jnp.float32)


def levels(key, shape, shards, smallest, largest):
    loudness = 1.0
    for dim, shards_of in shards:
        steps = jax.random.uniform(jax.random.fold_in(jax.random.fold_in(key, 6), dim), (shards_of,), jnp.float32, smallest / len(shards), largest / len(shards))
        loudness = loudness * jnp.repeat(jnp.exp(steps), shape[dim] // shards_of).reshape((-1,) + (1,) * (len(shape) - 1 - dim))
    return loudness


def normal_values(key, shape, scale, reach, cuts=(), dtype=jnp.bfloat16):
    drawn = jax.random.normal(key, shape, jnp.float32) * scale
    if len(cuts) > 0:
        drawn = levels(key, shape, cuts, -0.22, 0.18) * drawn
    return jnp.clip(drawn, min=-reach, max=reach).astype(dtype)


def setup_inputs(seed: int = 0) -> dict:
    keys = jax.random.split(jax.random.key(seed), 5)
    return {
        "left_panel": normal_values(keys[0], (M, NL), 1.0, 6.0, ((0, 8), (1, 4)), jnp.float32),
        "right_panel": normal_values(keys[1], (M, NR), M ** -0.5, 0.09375, ((0, 4), (1, 8)), jnp.float32),
        "arc_basis": draw_arc_basis(jax.random.fold_in(keys[4], 71), 0),
        "normal_block": normal_values(keys[3], (NL, NR), 1.0, 6.0, ((0, 4), (1, 8)), jnp.float32),
    }


def reference(left_panel, right_panel, arc_basis, normal_block):
    highest = lax.Precision.HIGHEST
    left_coef = jnp.dot(arc_basis.T.astype(jnp.float32), left_panel.astype(jnp.float32), precision=highest, preferred_element_type=jnp.float32)
    right_coef = jnp.dot(arc_basis.T.astype(jnp.float32), right_panel.astype(jnp.float32), precision=highest, preferred_element_type=jnp.float32)
    left_reduced = left_panel - jnp.dot(arc_basis.astype(jnp.float32), left_coef.astype(jnp.float32), precision=highest, preferred_element_type=jnp.float32)
    right_reduced = right_panel - jnp.dot(arc_basis.astype(jnp.float32), right_coef.astype(jnp.float32), precision=highest, preferred_element_type=jnp.float32)
    updated_block = normal_block + jnp.dot(left_reduced.T.astype(jnp.float32), right_reduced.astype(jnp.float32), precision=highest, preferred_element_type=jnp.float32)
    return (updated_block, left_reduced, right_reduced)
```

```python
import functools

import jax
import jax.numpy as jnp
from jax import lax
from jax.experimental import pallas as pl
from jax.experimental.pallas import tpu as pltpu
from jax.sharding import PartitionSpec as P

COMM = True
COMPUTE = True
STEPS = 32
AHEAD = 2
MT = 768

MESH = pl.DeviceIdType.MESH
F32 = jnp.float32
BF16 = jnp.bfloat16


def split(x):
    hi = x.astype(BF16)
    lo = (x - hi.astype(F32)).astype(BF16)
    return hi, lo


def kernel(
    steps, left, right, basis, block, acc_o, lct_o, rc_o, lg, rg,
    acc, lbuf, rbuf, qv, lt3, r3,
    s_own, s_relay, s_fwd, s_right, r_left, r_fwd, r_right, ld_sem, misc,
):
    r = lax.axis_index("row")
    c = lax.axis_index("col")
    z = c // 2
    k = c % 2
    sib = c + 1 - 2 * k
    rx = r + 1 - 2 * (r % 2)
    ry = (r + 2) % 4
    lr = lbuf.shape[3]
    nl = left.shape[1]
    nr = right.shape[2]
    ka = basis.shape[2]

    def remote(src, dst, ss, rs, row, col):
        return pltpu.make_async_remote_copy(
            src_ref=src, dst_ref=dst, send_sem=ss, recv_sem=rs,
            device_id={"row": row, "col": col}, device_id_type=MESH,
        )

    def mine(s):
        return left.at[pl.ds(pl.multiple_of(s * lr, lr), lr), :]

    def own_up(s):
        return remote(mine(s), lg.at[s, c], s_own.at[s, 0], r_left.at[s, z], r, c + 2)

    def own_dn(s):
        return remote(mine(s), lg.at[s, c], s_own.at[s, 1], r_left.at[s, z], r, c - 2)

    def own_far(s):
        far = 6 + k - 6 * (z // 3)
        return remote(mine(s), lg.at[s, c], s_own.at[s, 2], r_left.at[s, z], r, far)

    def relay_up(s):
        return remote(lg.at[s, c - 2], lg.at[s, c - 2], s_relay.at[s, 0], r_left.at[s, z - 1], r, c + 2)

    def relay_dn(s):
        return remote(lg.at[s, c + 2], lg.at[s, c + 2], s_relay.at[s, 1], r_left.at[s, z + 1], r, c - 2)

    def fwd_own(s):
        return remote(mine(s), lg.at[s, c], s_fwd.at[s, z], r_fwd.at[s, z], r, sib)

    def fwd(s, o):
        at = lg.at[s, 2 * o + k]
        return remote(at, at, s_fwd.at[s, o], r_fwd.at[s, o], r, sib)

    def arrived(s, o):
        at = lg.at[s, 2 * o + k]
        return remote(at, at, s_fwd.at[s, o], r_left.at[s, o], r, sib)

    def own_r(s, i, row):
        src = right.at[:, pl.ds(pl.multiple_of(s * lr, lr), lr), :]
        return remote(src, rg.at[s, r], s_right.at[s, i], r_right.at[s, i], row, c)

    def relay_r(s, i, owner, row):
        at = rg.at[s, owner, i]
        return remote(at, at, s_right.at[s, 2 + i], r_right.at[s, 2 + i], row, c)

    def start_own(s):
        own_r(s, 0, rx).start()
        own_r(s, 1, ry).start()

        @pl.when(z < 3)
        def _():
            own_up(s).start()

        @pl.when(z > 0)
        def _():
            own_dn(s).start()

        @pl.when(z % 3 == 0)
        def _():
            own_far(s).start()

        fwd_own(s).start()

    def stage1(s):
        own_r(s, 0, rx).wait_recv()
        relay_r(s, 0, rx, ry).start()
        own_r(s, 1, ry).wait_recv()
        relay_r(s, 1, ry, rx).start()

        @pl.when(z > 0)
        def _():
            arrived(s, z - 1).wait_recv()

            @pl.when(z < 3)
            def _():
                relay_up(s).start()

            fwd(s, z - 1).start()

        @pl.when(z < 3)
        def _():
            arrived(s, z + 1).wait_recv()

            @pl.when(z > 0)
            def _():
                relay_dn(s).start()

            fwd(s, z + 1).start()

    def stage2(s):
        far = (z + 2) % 4
        arrived(s, far).wait_recv()
        fwd(s, far).start()

        @pl.when(z % 3 == 0)
        def _():
            end = 3 - z
            arrived(s, end).wait_recv()
            fwd(s, end).start()

        relay_r(s, 0, rx, ry).wait_recv()
        relay_r(s, 1, ry, rx).wait_recv()

    def stage3(s):
        @pl.loop(0, 4)
        def _(o):
            at = lg.at[s, 2 * o + 1 - k]
            remote(at, at, s_fwd.at[s, o], r_fwd.at[s, o], r, sib).wait_recv()

    def load(s):
        slot = (s // 2) % 2
        i = s % 2
        pltpu.make_async_copy(mine(s), lbuf.at[slot, i, c], ld_sem.at[0, slot, i]).start()
        src = right.at[:, pl.ds(pl.multiple_of(s * lr, lr), lr), :]
        pltpu.make_async_copy(src, rbuf.at[slot, i, r], ld_sem.at[1, slot, i]).start()

        @pl.loop(1, 8)
        def _(d):
            o = (c + d) % 8
            pltpu.make_async_copy(lg.at[s, o], lbuf.at[slot, i, o], ld_sem.at[0, slot, i]).start()

        @pl.loop(1, 4)
        def _(d):
            o = (r + d) % 4
            pltpu.make_async_copy(rg.at[s, o], rbuf.at[slot, i, o], ld_sem.at[1, slot, i]).start()

    def loaded(s):
        slot = (s // 2) % 2
        i = s % 2
        pltpu.make_async_copy(lg.at[s], lbuf.at[slot, i], ld_sem.at[0, slot, i]).wait()
        pltpu.make_async_copy(rg.at[s], rbuf.at[slot, i], ld_sem.at[1, slot, i]).wait()

    depth = 2 * 8 * lr

    def put_left(x, at):
        hi, lo = split(x.T)
        lt3[pl.ds(at, 256), 0:depth] = hi
        lt3[pl.ds(at, 256), depth : 2 * depth] = lo
        lt3[pl.ds(at, 256), 2 * depth : 3 * depth] = hi

    def put_right(x, at):
        hi, lo = split(x)
        r3[0:depth, pl.ds(at, 256)] = hi
        r3[depth : 2 * depth, pl.ds(at, 256)] = hi
        r3[2 * depth : 3 * depth, pl.ds(at, 256)] = lo

    def prepare(j):
        slot = j % 2

        @pl.loop(0, nl // 256)
        def _(b):
            at = pl.multiple_of(b * 256, 256)
            put_left(lbuf[slot, :, :, :, pl.ds(at, 256)].reshape(depth, 256), at)

        @pl.loop(0, nr // 256)
        def _(b):
            at = pl.multiple_of(b * 256, 256)
            put_right(rbuf[slot, :, :, :, :, pl.ds(at, 256)].reshape(depth, 256), at)

        s = 2 * j
        q0 = qv[:, pl.ds(pl.multiple_of(s * lr, lr), lr), :].reshape(depth // 2, ka)
        q1 = qv[:, pl.ds(pl.multiple_of((s + 1) * lr, lr), lr), :].reshape(depth // 2, ka)
        q = jnp.concatenate([q0, q1], axis=0)
        put_left(q, nl)
        put_right(q, nr)

    tiles_n = (nr + ka) // 256
    tiles_m = (nl + ka) // MT

    def product(first, last):
        @pl.loop(first, last)
        def _(n):
            col = pl.multiple_of(n * 256, 256)

            @pl.loop(0, tiles_m)
            def _(m):
                row = pl.multiple_of(m * MT, 256)
                acc[pl.ds(row, MT), pl.ds(col, 256)] += jnp.dot(
                    lt3[pl.ds(row, MT), :], r3[:, pl.ds(col, 256)],
                    preferred_element_type=F32,
                )

    if COMM:
        barrier = pltpu.get_barrier_semaphore()
        za = (z + 1) % 4
        zb = (z + 3) % 4
        for row, col in ((rx, c), (ry, c), (r, sib), (r, 2 * za + k), (r, 2 * zb + k)):
            pl.semaphore_signal(barrier, inc=1, device_id={"row": row, "col": col}, device_id_type=MESH)
        pl.semaphore_wait(barrier, 5)
        for s in range(AHEAD):
            start_own(s)

    fill = pltpu.make_async_copy(block, acc.at[0:nl, 0:nr], misc.at[0])
    fill.start()
    qfill = pltpu.make_async_copy(basis, qv, misc.at[1])
    qfill.start()
    acc[nl:, :] = jnp.zeros((ka, nr + ka), F32)
    acc[0:nl, nr:] = jnp.zeros((nl, ka), F32)
    fill.wait()
    qfill.wait()

    half = tiles_n // 2
    lag = 3

    @pl.loop(0, steps + lag + 2)
    def _(t):
        if COMM:
            @pl.when(t + AHEAD < steps)
            def _():
                start_own(t + AHEAD)

            @pl.when(t < steps)
            def _():
                stage1(t)

            @pl.when((t >= 1) & (t < steps + 1))
            def _():
                stage2(t - 1)

            @pl.when((t >= 2) & (t < steps + 2))
            def _():
                stage3(t - 2)

        if COMPUTE:
            @pl.when((t >= 2) & (t < steps + 2))
            def _():
                load(t - 2)

            u = t - lag

            @pl.when((u >= 1) & (u < steps + 1) & (u % 2 == 1))
            def _():
                loaded(u - 1)
                loaded(u)
                prepare(u // 2)
                product(0, half)

            @pl.when((u >= 2) & (u < steps + 2) & (u % 2 == 0))
            def _():
                product(half, tiles_n)

    outs = [
        pltpu.make_async_copy(acc.at[0:nl, 0:nr], acc_o, misc.at[0]),
        pltpu.make_async_copy(acc.at[0:nl, nr:], lct_o, misc.at[1]),
        pltpu.make_async_copy(acc.at[nl:, 0:nr], rc_o, misc.at[2]),
    ]
    for out in outs:
        out.start()

    if COMM:
        @pl.loop(0, steps)
        def _(s):
            own_r(s, 0, rx).wait_send()
            own_r(s, 1, ry).wait_send()
            relay_r(s, 0, rx, ry).wait_send()
            relay_r(s, 1, ry, rx).wait_send()
            fwd_own(s).wait_send()

            @pl.loop(1, 4)
            def _(d):
                fwd(s, (z + d) % 4).wait_send()

            @pl.when(z < 3)
            def _():
                own_up(s).wait_send()

            @pl.when(z > 0)
            def _():
                own_dn(s).wait_send()

            @pl.when(z % 3 == 0)
            def _():
                own_far(s).wait_send()

            @pl.when((z > 0) & (z < 3))
            def _():
                relay_up(s).wait_send()
                relay_dn(s).wait_send()

    for out in outs:
        out.wait()


def gather_product(left, right, basis, block, rows, cols):
    steps = STEPS
    ml, nl = left.shape
    mr, nr = right.shape
    ka = basis.shape[1]
    lr = ml // steps
    right3 = right.reshape(cols // rows, ml, nr)
    basis3 = basis.reshape(cols, ml, ka)
    any_spec = pl.BlockSpec(memory_space=pl.ANY)
    dma = pltpu.SemaphoreType.DMA
    return pl.pallas_call(
        functools.partial(kernel, steps),
        out_shape=(
            jax.ShapeDtypeStruct((nl, nr), F32),
            jax.ShapeDtypeStruct((nl, ka), F32),
            jax.ShapeDtypeStruct((ka, nr), F32),
            jax.ShapeDtypeStruct((steps, cols, lr, nl), F32),
            jax.ShapeDtypeStruct((steps, rows, cols // rows, lr, nr), F32),
        ),
        in_specs=[any_spec] * 4,
        out_specs=[any_spec] * 5,
        scratch_shapes=[
            pltpu.VMEM((nl + ka, nr + ka), F32),
            pltpu.VMEM((2, 2, cols, lr, nl), F32),
            pltpu.VMEM((2, 2, rows, cols // rows, lr, nr), F32),
            pltpu.VMEM((cols, ml, ka), F32),
            pltpu.VMEM((nl + ka, 6 * cols * lr), BF16),
            pltpu.VMEM((6 * cols * lr, nr + ka), BF16),
            dma((steps, 3)),
            dma((steps, 2)),
            dma((steps, 4)),
            dma((steps, 4)),
            dma((steps, 4)),
            dma((steps, 4)),
            dma((steps, 4)),
            dma((2, 2, 2)),
            dma((3,)),
        ],
        compiler_params=pltpu.CompilerParams(
            collective_id=0, has_side_effects=True, vmem_limit_bytes=64000 * 1024
        ),
        name="gather_product",
    )(left, right3, basis3, block)


def dot(a, b, dims):
    return lax.dot_general(
        a, b, (dims, ((), ())), precision=lax.Precision.HIGH, preferred_element_type=F32
    )


def fast(rows, cols, left, right, basis, block):
    acc, lct, rc, _, _ = gather_product(left, right, basis, block, rows, cols)
    ml = left.shape[0]
    mr = right.shape[0]
    bl = lax.dynamic_slice_in_dim(basis, lax.axis_index("col") * ml, ml, 0)
    br = lax.dynamic_slice_in_dim(basis, lax.axis_index("row") * mr, mr, 0)
    updated = acc - dot(lct, rc, ((1,), (0,)))
    left_reduced = left - dot(bl, lct, ((1,), (1,)))
    right_reduced = right - dot(br, rc, ((1,), (0,)))
    return updated, left_reduced, right_reduced


def plain(left, right, basis, block):
    ml = left.shape[0]
    mr = right.shape[0]
    whole_left = lax.all_gather(left, "col", axis=0, tiled=True)
    whole_right = lax.all_gather(right, "row", axis=0, tiled=True)
    bl = lax.dynamic_slice_in_dim(basis, lax.axis_index("col") * ml, ml, 0)
    br = lax.dynamic_slice_in_dim(basis, lax.axis_index("row") * mr, mr, 0)
    lc = dot(basis, whole_left, ((0,), (0,)))
    rc = dot(basis, whole_right, ((0,), (0,)))
    updated = block + dot(whole_left, whole_right, ((0,), (0,))) - dot(lc, rc, ((0,), (0,)))
    left_reduced = left - dot(bl, lc, ((1,), (0,)))
    right_reduced = right - dot(br, rc, ((1,), (0,)))
    return updated, left_reduced, right_reduced


def solution(mesh):
    rows, cols = mesh.shape["row"], mesh.shape["col"]
    local = functools.partial(fast, rows, cols) if (rows, cols) == (4, 8) else plain
    in_specs = (P("col", "row"), P("row", "col"), P(), P("row", "col"))
    out_specs = (P("row", "col"), P("col", "row"), P("row", "col"))
    return jax.shard_map(
        local, mesh=mesh, in_specs=in_specs, out_specs=out_specs, check_vma=False
    )
```

```python
import functools

import jax
import jax.numpy as jnp
from jax import lax
from jax.experimental import pallas as pl
from jax.experimental.pallas import tpu as pltpu
from jax.sharding import PartitionSpec as P

COMM = True
COMPUTE = True
STEPS = 64
GROUP = 4
AHEAD = 2
D2 = 3
D3 = 4
MT = 2304

MESH = pl.DeviceIdType.MESH
F32 = jnp.float32
BF16 = jnp.bfloat16


def split(x):
    hi = x.astype(BF16)
    lo = (x - hi.astype(F32)).astype(BF16)
    return hi, lo


def kernel(
    steps, left, right, basis, block, acc_o, lct_o, rc_o, lg, rg,
    acc, lbuf, rbuf, qv, lt3, r3,
    s_own, s_relay, s_fwd, s_right, r_left, r_fwd, r_right, ld_sem, misc, tail_sem, out_sem,
):
    r = lax.axis_index("row")
    c = lax.axis_index("col")
    z = c // 2
    k = c % 2
    sib = c + 1 - 2 * k
    rx = r + 1 - 2 * (r % 2)
    ry = (r + 2) % 4
    lr = lbuf.shape[3]
    nl = left.shape[1]
    nr = right.shape[2]
    ka = basis.shape[2]

    def remote(src, dst, ss, rs, row, col):
        return pltpu.make_async_remote_copy(
            src_ref=src, dst_ref=dst, send_sem=ss, recv_sem=rs,
            device_id={"row": row, "col": col}, device_id_type=MESH,
        )

    def mine(s):
        return left.at[pl.ds(pl.multiple_of(s * lr, lr), lr), :]

    def own_up(s):
        return remote(mine(s), lg.at[s, c], s_own.at[s, 0], r_left.at[s, z], r, c + 2)

    def own_dn(s):
        return remote(mine(s), lg.at[s, c], s_own.at[s, 1], r_left.at[s, z], r, c - 2)

    def own_far(s):
        far = 6 + k - 6 * (z // 3)
        return remote(mine(s), lg.at[s, c], s_own.at[s, 2], r_left.at[s, z], r, far)

    def relay_up(s):
        return remote(lg.at[s, c - 2], lg.at[s, c - 2], s_relay.at[s, 0], r_left.at[s, z - 1], r, c + 2)

    def relay_dn(s):
        return remote(lg.at[s, c + 2], lg.at[s, c + 2], s_relay.at[s, 1], r_left.at[s, z + 1], r, c - 2)

    def fwd_own(s):
        return remote(mine(s), lg.at[s, c], s_fwd.at[s, z], r_fwd.at[s, z], r, sib)

    def fwd(s, o):
        at = lg.at[s, 2 * o + k]
        return remote(at, at, s_fwd.at[s, o], r_fwd.at[s, o], r, sib)

    def arrived(s, o):
        at = lg.at[s, 2 * o + k]
        return remote(at, at, s_fwd.at[s, o], r_left.at[s, o], r, sib)

    def own_r(s, i, row):
        src = right.at[:, pl.ds(pl.multiple_of(s * lr, lr), lr), :]
        return remote(src, rg.at[s, r], s_right.at[s, i], r_right.at[s, i], row, c)

    def relay_r(s, i, owner, row):
        at = rg.at[s, owner, i]
        return remote(at, at, s_right.at[s, 2 + i], r_right.at[s, 2 + i], row, c)

    def start_own(s):
        own_r(s, 0, rx).start()
        own_r(s, 1, ry).start()

        @pl.when(z < 3)
        def _():
            own_up(s).start()

        @pl.when(z > 0)
        def _():
            own_dn(s).start()

        @pl.when(z % 3 == 0)
        def _():
            own_far(s).start()

        fwd_own(s).start()

    def stage1(s):
        own_r(s, 0, rx).wait_recv()
        relay_r(s, 0, rx, ry).start()
        own_r(s, 1, ry).wait_recv()
        relay_r(s, 1, ry, rx).start()

        @pl.when(z > 0)
        def _():
            arrived(s, z - 1).wait_recv()

            @pl.when(z < 3)
            def _():
                relay_up(s).start()

            fwd(s, z - 1).start()

        @pl.when(z < 3)
        def _():
            arrived(s, z + 1).wait_recv()

            @pl.when(z > 0)
            def _():
                relay_dn(s).start()

            fwd(s, z + 1).start()

    def stage2(s):
        far = (z + 2) % 4
        arrived(s, far).wait_recv()
        fwd(s, far).start()

        @pl.when(z % 3 == 0)
        def _():
            end = 3 - z
            arrived(s, end).wait_recv()
            fwd(s, end).start()

        relay_r(s, 0, rx, ry).wait_recv()
        relay_r(s, 1, ry, rx).wait_recv()

    def stage3(s):
        @pl.loop(0, 4)
        def _(o):
            at = lg.at[s, 2 * o + 1 - k]
            remote(at, at, s_fwd.at[s, o], r_fwd.at[s, o], r, sib).wait_recv()

    def load(s):
        slot = (s // GROUP) % 2
        i = s % GROUP
        pltpu.make_async_copy(mine(s), lbuf.at[slot, i, c], ld_sem.at[0, slot, i]).start()
        src = right.at[:, pl.ds(pl.multiple_of(s * lr, lr), lr), :]
        pltpu.make_async_copy(src, rbuf.at[slot, i, r], ld_sem.at[1, slot, i]).start()

        @pl.loop(1, 8)
        def _(d):
            o = (c + d) % 8
            pltpu.make_async_copy(lg.at[s, o], lbuf.at[slot, i, o], ld_sem.at[0, slot, i]).start()

        @pl.loop(1, 4)
        def _(d):
            o = (r + d) % 4
            pltpu.make_async_copy(rg.at[s, o], rbuf.at[slot, i, o], ld_sem.at[1, slot, i]).start()

    def loaded(s):
        slot = (s // GROUP) % 2
        i = s % GROUP
        pltpu.make_async_copy(lg.at[s], lbuf.at[slot, i], ld_sem.at[0, slot, i]).wait()
        pltpu.make_async_copy(rg.at[s], rbuf.at[slot, i], ld_sem.at[1, slot, i]).wait()

    depth = GROUP * 8 * lr

    def put_left(x, at):
        hi, lo = split(x.T)
        lt3[pl.ds(at, 256), 0:depth] = hi
        lt3[pl.ds(at, 256), depth : 2 * depth] = lo
        lt3[pl.ds(at, 256), 2 * depth : 3 * depth] = hi

    def put_right(x, at):
        hi, lo = split(x)
        r3[0:depth, pl.ds(at, 256)] = hi
        r3[depth : 2 * depth, pl.ds(at, 256)] = hi
        r3[2 * depth : 3 * depth, pl.ds(at, 256)] = lo

    def prepare(j):
        slot = j % 2

        @pl.loop(0, nl // 256)
        def _(b):
            at = pl.multiple_of(b * 256, 256)
            put_left(lbuf[slot, :, :, :, pl.ds(at, 256)].reshape(depth, 256), at)

        @pl.loop(0, nr // 256)
        def _(b):
            at = pl.multiple_of(b * 256, 256)
            put_right(rbuf[slot, :, :, :, :, pl.ds(at, 256)].reshape(depth, 256), at)

        q = qv[:, pl.ds(pl.multiple_of(j * GROUP * lr, GROUP * lr), GROUP * lr), :]
        q = jnp.concatenate(
            [q[:, i * lr : (i + 1) * lr].reshape(8 * lr, ka) for i in range(GROUP)], axis=0
        )
        put_left(q, nl)
        put_right(q, nr)

    tiles_n = (nr + ka) // 256
    tiles_m = (nl + ka) // MT

    def product(first, last):
        @pl.loop(first, last)
        def _(n):
            col = pl.multiple_of(n * 256, 256)

            @pl.loop(0, tiles_m)
            def _(m):
                row = pl.multiple_of(m * MT, 256)
                acc[pl.ds(row, MT), pl.ds(col, 256)] += jnp.dot(
                    lt3[pl.ds(row, MT), :], r3[:, pl.ds(col, 256)],
                    preferred_element_type=F32,
                )

    if True:
        barrier = pltpu.get_barrier_semaphore()
        za = (z + 1) % 4
        zb = (z + 3) % 4
        for row, col in ((rx, c), (ry, c), (r, sib), (r, 2 * za + k), (r, 2 * zb + k)):
            pl.semaphore_signal(barrier, inc=1, device_id={"row": row, "col": col}, device_id_type=MESH)
        pl.semaphore_wait(barrier, 5)
    if COMM:
        for s in range(AHEAD):
            start_own(s)

    fill = pltpu.make_async_copy(block, acc.at[0:nl, 0:nr], misc.at[0])
    fill.start()
    qfill = pltpu.make_async_copy(basis, qv, misc.at[1])
    qfill.start()
    acc[nl:, :] = jnp.zeros((ka, nr + ka), F32)
    acc[0:nl, nr:] = jnp.zeros((nl, ka), F32)

    first = steps - GROUP
    for i in range(GROUP):
        rows = pl.ds((first + i) * lr, lr)
        own = (
            pltpu.make_async_copy(left.at[rows, :], lbuf.at[1, i, c], tail_sem.at[0, i]),
            pltpu.make_async_copy(right.at[:, rows, :], rbuf.at[1, i, r], tail_sem.at[1, i]),
        )
        for copy in own:
            copy.start()
        for copy in own:
            copy.wait()
        own = (
            pltpu.make_async_copy(lbuf.at[1, i, c], lg.at[first + i, c], tail_sem.at[0, i]),
            pltpu.make_async_copy(rbuf.at[1, i, r], rg.at[first + i, r], tail_sem.at[1, i]),
        )
        for copy in own:
            copy.start()
        for copy in own:
            copy.wait()
    fill.wait()
    qfill.wait()

    groups = steps // GROUP - 1
    cuts = (0, tiles_n // 8, tiles_n // 2, (7 * tiles_n + 7) // 9, tiles_n)

    def out_tile(n):
        cols = pl.ds(pl.multiple_of(n * 256, 256), 256)
        return pltpu.make_async_copy(acc.at[0:nl, cols], acc_o.at[:, cols], out_sem.at[n])

    @pl.loop(0, steps + D3)
    def _(t):
        if COMM:
            @pl.when(t + AHEAD < steps)
            def _():
                start_own(t + AHEAD)

            @pl.when(t < steps)
            def _():
                stage1(t)

            @pl.when((t >= D2) & (t < steps + D2))
            def _():
                stage2(t - D2)

            @pl.when(t >= D3)
            def _():
                stage3(t - D3)

        if COMPUTE:
            @pl.when((t >= D3) & (t < groups * GROUP + D3))
            def _():
                load(t - D3)

            v = t - D3 - GROUP
            j = v // GROUP

            @pl.when((v >= 0) & (v % GROUP == 0))
            def _():
                for i in range(GROUP):
                    loaded(v + i)
                prepare(j)

            for q in range(GROUP):
                @pl.when((v >= 0) & (v % GROUP == q))
                def _():
                    product(cuts[q], cuts[q + 1])

                    @pl.when(j == groups - 1)
                    def _():
                        @pl.loop(cuts[q], min(cuts[q + 1], nr // 256))
                        def _(n):
                            out_tile(n).start()

    outs = [
        pltpu.make_async_copy(acc.at[0:nl, nr:], lct_o, misc.at[1]),
        pltpu.make_async_copy(acc.at[nl:, 0:nr], rc_o, misc.at[2]),
    ]
    for out in outs:
        out.start()

    if COMM:
        @pl.loop(0, steps)
        def _(s):
            own_r(s, 0, rx).wait_send()
            own_r(s, 1, ry).wait_send()
            relay_r(s, 0, rx, ry).wait_send()
            relay_r(s, 1, ry, rx).wait_send()
            fwd_own(s).wait_send()

            @pl.loop(1, 4)
            def _(d):
                fwd(s, (z + d) % 4).wait_send()

            @pl.when(z < 3)
            def _():
                own_up(s).wait_send()

            @pl.when(z > 0)
            def _():
                own_dn(s).wait_send()

            @pl.when(z % 3 == 0)
            def _():
                own_far(s).wait_send()

            @pl.when((z > 0) & (z < 3))
            def _():
                relay_up(s).wait_send()
                relay_dn(s).wait_send()

    for out in outs:
        out.wait()
    if COMPUTE:
        @pl.loop(0, nr // 256)
        def _(n):
            out_tile(n).wait()


def gather_product(left, right, basis, block, rows, cols):
    steps = STEPS
    ml, nl = left.shape
    mr, nr = right.shape
    ka = basis.shape[1]
    lr = ml // steps
    right3 = right.reshape(cols // rows, ml, nr)
    basis3 = basis.reshape(cols, ml, ka)
    any_spec = pl.BlockSpec(memory_space=pl.ANY)
    dma = pltpu.SemaphoreType.DMA
    return pl.pallas_call(
        functools.partial(kernel, steps),
        out_shape=(
            jax.ShapeDtypeStruct((nl, nr), F32),
            jax.ShapeDtypeStruct((nl, ka), F32),
            jax.ShapeDtypeStruct((ka, nr), F32),
            jax.ShapeDtypeStruct((steps, cols, lr, nl), F32),
            jax.ShapeDtypeStruct((steps, rows, cols // rows, lr, nr), F32),
        ),
        in_specs=[any_spec] * 4,
        out_specs=[any_spec] * 5,
        scratch_shapes=[
            pltpu.VMEM((nl + ka, nr + ka), F32),
            pltpu.VMEM((2, GROUP, cols, lr, nl), F32),
            pltpu.VMEM((2, GROUP, rows, cols // rows, lr, nr), F32),
            pltpu.VMEM((cols, ml, ka), F32),
            pltpu.VMEM((nl + ka, 3 * GROUP * cols * lr), BF16),
            pltpu.VMEM((3 * GROUP * cols * lr, nr + ka), BF16),
            dma((steps, 3)),
            dma((steps, 2)),
            dma((steps, 4)),
            dma((steps, 4)),
            dma((steps, 4)),
            dma((steps, 4)),
            dma((steps, 4)),
            dma((2, 2, GROUP)),
            dma((3,)),
            dma((2, GROUP)),
            dma((nr // 256,)),
        ],
        compiler_params=pltpu.CompilerParams(
            collective_id=0, has_side_effects=True, vmem_limit_bytes=64000 * 1024
        ),
        name="gather_product",
    )(left, right3, basis3, block)


def dot(a, b, dims):
    return lax.dot_general(
        a, b, (dims, ((), ())), precision=lax.Precision.HIGH, preferred_element_type=F32
    )


def finish_kernel(
    acc, lct, rc, lg, rg, qt, left, right, ql, qr, out, left_o, right_o,
    lt3, qth, qtl, qls, qrs,
):
    n = pl.program_id(0)
    group, parts, lr = lg.shape[0], lg.shape[1], lg.shape[2]
    depth = group * parts * lr
    nl, ka = lct.shape
    mm = functools.partial(jnp.dot, preferred_element_type=F32)

    def nt(a, b):
        return lax.dot_general(a, b, (((1,), (1,)), ((), ())), preferred_element_type=F32)

    @pl.when(n == 0)
    def _():
        q = jnp.concatenate(
            [qt[:, i * lr : (i + 1) * lr].reshape(parts * lr, ka) for i in range(group)], axis=0
        )
        qh, qlo = split(q)
        hi, lo = split(q.T)
        qth[...] = hi
        qtl[...] = lo
        hi, lo = split(ql[0])
        qls[:, 0:ka] = hi
        qls[:, ka:] = lo
        hi, lo = split(qr[0])
        qrs[:, 0:ka] = hi
        qrs[:, ka:] = lo

        @pl.loop(0, nl // 256)
        def _(b):
            at = pl.ds(pl.multiple_of(b * 256, 256), 256)
            hi, lo = split(lg[:, :, :, at].reshape(depth, 256).T)
            lt3[at, 0:depth] = hi
            lt3[at, depth : 2 * depth] = lo
            lt3[at, 2 * depth : 3 * depth] = hi
            coef = lct[at, :] + (mm(hi, qh) + mm(lo, qh) + mm(hi, qlo))
            hi, lo = split(-coef)
            base = 3 * depth
            lt3[at, base : base + ka] = hi
            lt3[at, base + ka : base + 2 * ka] = lo
            lt3[at, base + 2 * ka :] = hi

    y = rg[...].reshape(depth, rg.shape[-1])
    yh, yl = split(y)
    coef = rc[...] + (mm(qth[...], yh) + mm(qtl[...], yh) + mm(qth[...], yl))
    ch, cl = split(coef)
    r3 = jnp.concatenate([yh, yh, yl, ch, ch, cl], axis=0)
    out[...] = acc[...] + mm(lt3[...], r3)
    qh, qlo = qrs[:, 0:ka], qrs[:, ka:]
    right_o[...] = right[...] - (mm(qh, ch) + mm(qlo, ch) + mm(qh, cl))
    at = pl.ds(pl.multiple_of(n * 256, 256), 256)
    base = 3 * depth
    lh = lt3[at, base : base + ka]
    ll = lt3[at, base + ka : base + 2 * ka]
    qh, qlo = qls[:, 0:ka], qls[:, ka:]
    left_o[...] = left[...] + (nt(qh, lh) + nt(qlo, lh) + nt(qh, ll))


def finish(acc, lct, rc, lg, rg, left, right, basis, rows, cols):
    ml, nl = left.shape
    mr, nr = right.shape
    ka = basis.shape[1]
    steps, _, lr, _ = lg.shape
    last = steps // GROUP - 1
    depth = GROUP * cols * lr
    basis3 = basis.reshape(cols, ml, ka)
    basis4 = basis.reshape(rows, mr, ka)
    ql = lax.dynamic_index_in_dim(basis3, lax.axis_index("col"), 0)
    qr = lax.dynamic_index_in_dim(basis4, lax.axis_index("row"), 0)
    tile = lambda height: pl.BlockSpec((height, 256), lambda n: (0, n))
    once = lambda shape, index: pl.BlockSpec(shape, lambda n: index, pipeline_mode=pl.Buffered(1))
    return pl.pallas_call(
        finish_kernel,
        grid=(nr // 256,),
        out_shape=(
            jax.ShapeDtypeStruct((nl, nr), F32),
            jax.ShapeDtypeStruct((ml, nl), F32),
            jax.ShapeDtypeStruct((mr, nr), F32),
        ),
        in_specs=[
            tile(nl),
            once((nl, ka), (0, 0)),
            tile(ka),
            once((GROUP, cols, lr, nl), (last, 0, 0, 0)),
            pl.BlockSpec((GROUP, rows, cols // rows, lr, 256), lambda n: (last, 0, 0, 0, n)),
            once((cols, GROUP * lr, ka), (0, last, 0)),
            tile(ml),
            tile(mr),
            once((1, ml, ka), (0, 0, 0)),
            once((1, mr, ka), (0, 0, 0)),
        ],
        out_specs=[tile(nl), tile(ml), tile(mr)],
        scratch_shapes=[
            pltpu.VMEM((nl, 3 * depth + 3 * ka), BF16),
            pltpu.VMEM((ka, depth), BF16),
            pltpu.VMEM((ka, depth), BF16),
            pltpu.VMEM((ml, 2 * ka), BF16),
            pltpu.VMEM((mr, 2 * ka), BF16),
        ],
        compiler_params=pltpu.CompilerParams(
            dimension_semantics=("arbitrary",), vmem_limit_bytes=60000 * 1024
        ),
        name="finish",
    )(acc, lct, rc, lg, rg, basis3, left, right, ql, qr)


def fast(rows, cols, left, right, basis, block):
    acc, lct, rc, lg, rg = gather_product(left, right, basis, block, rows, cols)
    return finish(acc, lct, rc, lg, rg, left, right, basis, rows, cols)


def plain(left, right, basis, block):
    ml = left.shape[0]
    mr = right.shape[0]
    whole_left = lax.all_gather(left, "col", axis=0, tiled=True)
    whole_right = lax.all_gather(right, "row", axis=0, tiled=True)
    bl = lax.dynamic_slice_in_dim(basis, lax.axis_index("col") * ml, ml, 0)
    br = lax.dynamic_slice_in_dim(basis, lax.axis_index("row") * mr, mr, 0)
    lc = dot(basis, whole_left, ((0,), (0,)))
    rc = dot(basis, whole_right, ((0,), (0,)))
    updated = block + dot(whole_left, whole_right, ((0,), (0,))) - dot(lc, rc, ((0,), (0,)))
    left_reduced = left - dot(bl, lc, ((1,), (0,)))
    right_reduced = right - dot(br, rc, ((1,), (0,)))
    return updated, left_reduced, right_reduced


def solution(mesh):
    rows, cols = mesh.shape["row"], mesh.shape["col"]
    local = functools.partial(fast, rows, cols) if (rows, cols) == (4, 8) else plain
    in_specs = (P("col", "row"), P("row", "col"), P(), P("row", "col"))
    out_specs = (P("row", "col"), P("col", "row"), P("row", "col"))
    return jax.shard_map(
        local, mesh=mesh, in_specs=in_specs, out_specs=out_specs, check_vma=False
    )
```

```python
import functools

import jax
import jax.numpy as jnp
from jax import lax
from jax.experimental import pallas as pl
from jax.experimental.pallas import tpu as pltpu
from jax.sharding import PartitionSpec as P

COMM = True
COMPUTE = True
STEPS = 32
GROUP = 2
AHEAD = 1
D2 = 1
D3 = 2
TRAIL = 0
CUTS = (0, 4, 9)

MESH = pl.DeviceIdType.MESH
F32 = jnp.float32
BF16 = jnp.bfloat16


def split(x):
    hi = x.astype(BF16)
    lo = (x - hi.astype(F32)).astype(BF16)
    return hi, lo


def kernel(
    steps, left, right, basis, block, acc_o, lct_o, rc_o, lg, rg,
    acc, lbuf, rbuf, qv, lt3, r3, ltail, rtail,
    s_own, s_relay, s_fwd, s_right, r_left, r_fwd, r_right, ld_sem, misc, tail_sem, out_sem,
):
    r = lax.axis_index("row")
    c = lax.axis_index("col")
    z = c // 2
    k = c % 2
    sib = c + 1 - 2 * k
    rx = r + 1 - 2 * (r % 2)
    ry = (r + 2) % 4
    lr = lbuf.shape[3]
    nl = left.shape[1]
    nr = right.shape[2]
    ka = basis.shape[2]

    def remote(src, dst, ss, rs, row, col):
        return pltpu.make_async_remote_copy(
            src_ref=src, dst_ref=dst, send_sem=ss, recv_sem=rs,
            device_id={"row": row, "col": col}, device_id_type=MESH,
        )

    def mine(s):
        return left.at[pl.ds(pl.multiple_of(s * lr, lr), lr), :]

    def own_up(s):
        return remote(mine(s), lg.at[s, c], s_own.at[s, 0], r_left.at[s, z], r, c + 2)

    def own_dn(s):
        return remote(mine(s), lg.at[s, c], s_own.at[s, 1], r_left.at[s, z], r, c - 2)

    def own_far(s):
        far = 6 + k - 6 * (z // 3)
        return remote(mine(s), lg.at[s, c], s_own.at[s, 2], r_left.at[s, z], r, far)

    def relay_up(s):
        return remote(lg.at[s, c - 2], lg.at[s, c - 2], s_relay.at[s, 0], r_left.at[s, z - 1], r, c + 2)

    def relay_dn(s):
        return remote(lg.at[s, c + 2], lg.at[s, c + 2], s_relay.at[s, 1], r_left.at[s, z + 1], r, c - 2)

    def fwd_own(s):
        return remote(mine(s), lg.at[s, c], s_fwd.at[s, z], r_fwd.at[s, z], r, sib)

    def fwd(s, o):
        at = lg.at[s, 2 * o + k]
        return remote(at, at, s_fwd.at[s, o], r_fwd.at[s, o], r, sib)

    def arrived(s, o):
        at = lg.at[s, 2 * o + k]
        return remote(at, at, s_fwd.at[s, o], r_left.at[s, o], r, sib)

    def own_r(s, i, row):
        src = right.at[:, pl.ds(pl.multiple_of(s * lr, lr), lr), :]
        return remote(src, rg.at[s, r], s_right.at[s, i], r_right.at[s, i], row, c)

    def relay_r(s, i, owner, row):
        at = rg.at[s, owner, i]
        return remote(at, at, s_right.at[s, 2 + i], r_right.at[s, 2 + i], row, c)

    def start_own(s):
        own_r(s, 0, rx).start()
        own_r(s, 1, ry).start()

        @pl.when(z < 3)
        def _():
            own_up(s).start()

        @pl.when(z > 0)
        def _():
            own_dn(s).start()

        @pl.when(z % 3 == 0)
        def _():
            own_far(s).start()

        fwd_own(s).start()

    def stage1(s):
        own_r(s, 0, rx).wait_recv()
        relay_r(s, 0, rx, ry).start()
        own_r(s, 1, ry).wait_recv()
        relay_r(s, 1, ry, rx).start()

        @pl.when(z > 0)
        def _():
            arrived(s, z - 1).wait_recv()

            @pl.when(z < 3)
            def _():
                relay_up(s).start()

            fwd(s, z - 1).start()

        @pl.when(z < 3)
        def _():
            arrived(s, z + 1).wait_recv()

            @pl.when(z > 0)
            def _():
                relay_dn(s).start()

            fwd(s, z + 1).start()

    def stage2(s):
        far = (z + 2) % 4
        arrived(s, far).wait_recv()
        fwd(s, far).start()

        @pl.when(z % 3 == 0)
        def _():
            end = 3 - z
            arrived(s, end).wait_recv()
            fwd(s, end).start()

        relay_r(s, 0, rx, ry).wait_recv()
        relay_r(s, 1, ry, rx).wait_recv()

    def stage3(s):
        @pl.loop(0, 4)
        def _(o):
            at = lg.at[s, 2 * o + 1 - k]
            remote(at, at, s_fwd.at[s, o], r_fwd.at[s, o], r, sib).wait_recv()

    def load(s):
        slot = (s // GROUP) % 2
        i = s % GROUP
        pltpu.make_async_copy(mine(s), lbuf.at[slot, i, c], ld_sem.at[0, slot, i]).start()
        src = right.at[:, pl.ds(pl.multiple_of(s * lr, lr), lr), :]
        pltpu.make_async_copy(src, rbuf.at[slot, i, r], ld_sem.at[1, slot, i]).start()

        @pl.loop(1, 8)
        def _(d):
            o = (c + d) % 8
            pltpu.make_async_copy(lg.at[s, o], lbuf.at[slot, i, o], ld_sem.at[0, slot, i]).start()

        @pl.loop(1, 4)
        def _(d):
            o = (r + d) % 4
            pltpu.make_async_copy(rg.at[s, o], rbuf.at[slot, i, o], ld_sem.at[1, slot, i]).start()

    def loaded(s):
        slot = (s // GROUP) % 2
        i = s % GROUP
        pltpu.make_async_copy(lg.at[s], lbuf.at[slot, i], ld_sem.at[0, slot, i]).wait()
        pltpu.make_async_copy(rg.at[s], rbuf.at[slot, i], ld_sem.at[1, slot, i]).wait()

    depth = GROUP * 8 * lr

    def put_left(x, at):
        hi, lo = split(x.T)
        lt3[pl.ds(at, 256), 0:depth] = hi
        lt3[pl.ds(at, 256), depth : 2 * depth] = lo
        lt3[pl.ds(at, 256), 2 * depth : 3 * depth] = hi

    def put_right(x, at):
        hi, lo = split(x)
        r3[0:depth, pl.ds(at, 256)] = hi
        r3[depth : 2 * depth, pl.ds(at, 256)] = hi
        r3[2 * depth : 3 * depth, pl.ds(at, 256)] = lo

    def prepare(j):
        slot = j % 2

        @pl.loop(0, nl // 256)
        def _(b):
            at = pl.multiple_of(b * 256, 256)
            put_left(lbuf[slot, :, :, :, pl.ds(at, 256)].reshape(depth, 256), at)

        @pl.loop(0, nr // 256)
        def _(b):
            at = pl.multiple_of(b * 256, 256)
            put_right(rbuf[slot, :, :, :, :, pl.ds(at, 256)].reshape(depth, 256), at)

        q = qv[:, pl.ds(pl.multiple_of(j * GROUP * lr, GROUP * lr), GROUP * lr), :]
        q = jnp.concatenate(
            [q[:, i * lr : (i + 1) * lr].reshape(8 * lr, ka) for i in range(GROUP)], axis=0
        )
        put_left(q, nl)
        put_right(q, nr)

    tiles_n = (nr + ka) // 256

    def product(first, last):
        @pl.loop(first, last)
        def _(n):
            cols = pl.ds(pl.multiple_of(n * 256, 256), 256)
            acc[:, cols] += jnp.dot(lt3[...], r3[:, cols], preferred_element_type=F32)

    if True:
        barrier = pltpu.get_barrier_semaphore()
        za = (z + 1) % 4
        zb = (z + 3) % 4
        for row, col in ((rx, c), (ry, c), (r, sib), (r, 2 * za + k), (r, 2 * zb + k)):
            pl.semaphore_signal(barrier, inc=1, device_id={"row": row, "col": col}, device_id_type=MESH)
        pl.semaphore_wait(barrier, 5)
    if COMM:
        for s in range(AHEAD):
            start_own(s)

    fill = pltpu.make_async_copy(block, acc.at[0:nl, 0:nr], misc.at[0])
    fill.start()
    qfill = pltpu.make_async_copy(basis, qv, misc.at[1])
    qfill.start()
    acc[nl:, :] = jnp.zeros((ka, nr + ka), F32)
    acc[0:nl, nr:] = jnp.zeros((nl, ka), F32)

    first = steps - GROUP
    tail_in = []
    tail_out = []
    for i in range(GROUP):
        at = pl.ds((first + i) * lr, lr)
        tail_in += [
            pltpu.make_async_copy(left.at[at, :], ltail.at[i], tail_sem.at[0, i]),
            pltpu.make_async_copy(right.at[:, at, :], rtail.at[i], tail_sem.at[1, i]),
        ]
        tail_out += [
            pltpu.make_async_copy(ltail.at[i], lg.at[first + i, c], tail_sem.at[2, i]),
            pltpu.make_async_copy(rtail.at[i], rg.at[first + i, r], tail_sem.at[3, i]),
        ]
    for copy in tail_in:
        copy.start()

    groups = steps // GROUP - 1
    cuts = [cut * tiles_n // CUTS[-1] for cut in CUTS]

    def out_tile(n):
        cols = pl.ds(pl.multiple_of(n * 256, 256), 256)
        return pltpu.make_async_copy(acc.at[0:nl, cols], acc_o.at[:, cols], out_sem.at[n])

    @pl.loop(0, steps + D3 + TRAIL)
    def _(t):
        if COMM:
            @pl.when(t + AHEAD < steps)
            def _():
                start_own(t + AHEAD)

        if COMPUTE:
            v = t - D3 - 1 - (GROUP - 1)
            j = v // GROUP

            @pl.when(v == 0)
            def _():
                fill.wait()
                qfill.wait()
                for copy in tail_in:
                    copy.wait()
                for copy in tail_out:
                    copy.start()

            for q in range(GROUP):
                @pl.when((v >= 0) & (v < groups * GROUP) & (v % GROUP == q))
                def _():
                    if q == 0:
                        for i in range(GROUP):
                            loaded(v + i)
                        prepare(j)
                    product(cuts[q], cuts[q + 1])

                    @pl.when(j == groups - 1)
                    def _():
                        @pl.loop(cuts[q], min(cuts[q + 1], nr // 256))
                        def _(n):
                            out_tile(n).start()

        if COMM:
            @pl.when((t >= D3) & (t < steps + D3))
            def _():
                stage3(t - D3)
        if COMPUTE:
            @pl.when((t >= D3) & (t < groups * GROUP + D3))
            def _():
                load(t - D3)
        if COMM:
            @pl.when(t < steps)
            def _():
                stage1(t)

            @pl.when((t >= D2) & (t < steps + D2))
            def _():
                stage2(t - D2)

    outs = [
        pltpu.make_async_copy(acc.at[0:nl, nr:], lct_o, misc.at[1]),
        pltpu.make_async_copy(acc.at[nl:, 0:nr], rc_o, misc.at[2]),
    ]
    for out in outs:
        out.start()

    if COMM:
        @pl.loop(0, steps)
        def _(s):
            own_r(s, 0, rx).wait_send()
            own_r(s, 1, ry).wait_send()
            relay_r(s, 0, rx, ry).wait_send()
            relay_r(s, 1, ry, rx).wait_send()
            fwd_own(s).wait_send()

            @pl.loop(1, 4)
            def _(d):
                fwd(s, (z + d) % 4).wait_send()

            @pl.when(z < 3)
            def _():
                own_up(s).wait_send()

            @pl.when(z > 0)
            def _():
                own_dn(s).wait_send()

            @pl.when(z % 3 == 0)
            def _():
                own_far(s).wait_send()

            @pl.when((z > 0) & (z < 3))
            def _():
                relay_up(s).wait_send()
                relay_dn(s).wait_send()

    for out in outs:
        out.wait()
    if not COMPUTE:
        for copy in tail_in + [fill, qfill]:
            copy.wait()
    if COMPUTE:
        for copy in tail_out:
            copy.wait()

        @pl.loop(0, nr // 256)
        def _(n):
            out_tile(n).wait()


def gather_product(left, right, basis, block, rows, cols):
    steps = STEPS
    ml, nl = left.shape
    mr, nr = right.shape
    ka = basis.shape[1]
    lr = ml // steps
    right3 = right.reshape(cols // rows, ml, nr)
    basis3 = basis.reshape(cols, ml, ka)
    any_spec = pl.BlockSpec(memory_space=pl.ANY)
    dma = pltpu.SemaphoreType.DMA
    return pl.pallas_call(
        functools.partial(kernel, steps),
        out_shape=(
            jax.ShapeDtypeStruct((nl, nr), F32),
            jax.ShapeDtypeStruct((nl, ka), F32),
            jax.ShapeDtypeStruct((ka, nr), F32),
            jax.ShapeDtypeStruct((steps, cols, lr, nl), F32),
            jax.ShapeDtypeStruct((steps, rows, cols // rows, lr, nr), F32),
        ),
        in_specs=[any_spec] * 4,
        out_specs=[any_spec] * 5,
        scratch_shapes=[
            pltpu.VMEM((nl + ka, nr + ka), F32),
            pltpu.VMEM((2, GROUP, cols, lr, nl), F32),
            pltpu.VMEM((2, GROUP, rows, cols // rows, lr, nr), F32),
            pltpu.VMEM((cols, ml, ka), F32),
            pltpu.VMEM((nl + ka, 3 * GROUP * cols * lr), BF16),
            pltpu.VMEM((3 * GROUP * cols * lr, nr + ka), BF16),
            pltpu.VMEM((GROUP, lr, nl), F32),
            pltpu.VMEM((GROUP, cols // rows, lr, nr), F32),
            dma((steps, 3)),
            dma((steps, 2)),
            dma((steps, 4)),
            dma((steps, 4)),
            dma((steps, 4)),
            dma((steps, 4)),
            dma((steps, 4)),
            dma((2, 2, GROUP)),
            dma((3,)),
            dma((4, GROUP)),
            dma((nr // 256,)),
        ],
        compiler_params=pltpu.CompilerParams(
            collective_id=0, has_side_effects=True, vmem_limit_bytes=64000 * 1024
        ),
        name="gather_product",
    )(left, right3, basis3, block)


def dot(a, b, dims):
    return lax.dot_general(
        a, b, (dims, ((), ())), precision=lax.Precision.HIGH, preferred_element_type=F32
    )


def finish_kernel(
    acc, lct, rc, lg, rg, qt, left, right, ql, qr, out, left_o, right_o,
    lt3, qth, qtl, qls, qrs,
):
    n = pl.program_id(0)
    group, parts, lr = lg.shape[0], lg.shape[1], lg.shape[2]
    depth = group * parts * lr
    nl, ka = lct.shape
    mm = functools.partial(jnp.dot, preferred_element_type=F32)

    def nt(a, b):
        return lax.dot_general(a, b, (((1,), (1,)), ((), ())), preferred_element_type=F32)

    @pl.when(n == 0)
    def _():
        q = jnp.concatenate(
            [qt[:, i * lr : (i + 1) * lr].reshape(parts * lr, ka) for i in range(group)], axis=0
        )
        qh, qlo = split(q)
        hi, lo = split(q.T)
        qth[...] = hi
        qtl[...] = lo
        hi, lo = split(ql[0])
        qls[:, 0:ka] = hi
        qls[:, ka:] = lo
        hi, lo = split(qr[0])
        qrs[:, 0:ka] = hi
        qrs[:, ka:] = lo

        @pl.loop(0, nl // 256)
        def _(b):
            at = pl.ds(pl.multiple_of(b * 256, 256), 256)
            hi, lo = split(lg[:, :, :, at].reshape(depth, 256).T)
            lt3[at, 0:depth] = hi
            lt3[at, depth : 2 * depth] = lo
            lt3[at, 2 * depth : 3 * depth] = hi
            coef = lct[at, :] + (mm(hi, qh) + mm(lo, qh) + mm(hi, qlo))
            hi, lo = split(-coef)
            base = 3 * depth
            lt3[at, base : base + ka] = hi
            lt3[at, base + ka : base + 2 * ka] = lo
            lt3[at, base + 2 * ka :] = hi

    y = rg[...].reshape(depth, rg.shape[-1])
    yh, yl = split(y)
    coef = rc[...] + (mm(qth[...], yh) + mm(qtl[...], yh) + mm(qth[...], yl))
    ch, cl = split(coef)
    r3 = jnp.concatenate([yh, yh, yl, ch, ch, cl], axis=0)
    out[...] = acc[...] + mm(lt3[...], r3)
    qh, qlo = qrs[:, 0:ka], qrs[:, ka:]
    right_o[...] = right[...] - (mm(qh, ch) + mm(qlo, ch) + mm(qh, cl))
    at = pl.ds(pl.multiple_of(n * 256, 256), 256)
    base = 3 * depth
    lh = lt3[at, base : base + ka]
    ll = lt3[at, base + ka : base + 2 * ka]
    qh, qlo = qls[:, 0:ka], qls[:, ka:]
    left_o[...] = left[...] + (nt(qh, lh) + nt(qlo, lh) + nt(qh, ll))


def finish(acc, lct, rc, lg, rg, left, right, basis, rows, cols):
    ml, nl = left.shape
    mr, nr = right.shape
    ka = basis.shape[1]
    steps, _, lr, _ = lg.shape
    last = steps // GROUP - 1
    depth = GROUP * cols * lr
    basis3 = basis.reshape(cols, ml, ka)
    basis4 = basis.reshape(rows, mr, ka)
    tile = lambda height: pl.BlockSpec((height, 256), lambda n: (0, n))
    once = lambda shape, index: pl.BlockSpec(shape, lambda n: index, pipeline_mode=pl.Buffered(1))
    return pl.pallas_call(
        finish_kernel,
        grid=(nr // 256,),
        out_shape=(
            jax.ShapeDtypeStruct((nl, nr), F32),
            jax.ShapeDtypeStruct((ml, nl), F32),
            jax.ShapeDtypeStruct((mr, nr), F32),
        ),
        in_specs=[
            tile(nl),
            once((nl, ka), (0, 0)),
            tile(ka),
            once((GROUP, cols, lr, nl), (last, 0, 0, 0)),
            pl.BlockSpec((GROUP, rows, cols // rows, lr, 256), lambda n: (last, 0, 0, 0, n)),
            once((cols, GROUP * lr, ka), (0, last, 0)),
            tile(ml),
            tile(mr),
            pl.BlockSpec((1, ml, ka), lambda n: (lax.axis_index("col"), 0, 0), pipeline_mode=pl.Buffered(1)),
            pl.BlockSpec((1, mr, ka), lambda n: (lax.axis_index("row"), 0, 0), pipeline_mode=pl.Buffered(1)),
        ],
        out_specs=[tile(nl), tile(ml), tile(mr)],
        scratch_shapes=[
            pltpu.VMEM((nl, 3 * depth + 3 * ka), BF16),
            pltpu.VMEM((ka, depth), BF16),
            pltpu.VMEM((ka, depth), BF16),
            pltpu.VMEM((ml, 2 * ka), BF16),
            pltpu.VMEM((mr, 2 * ka), BF16),
        ],
        compiler_params=pltpu.CompilerParams(
            dimension_semantics=("arbitrary",), vmem_limit_bytes=60000 * 1024
        ),
        name="finish",
    )(acc, lct, rc, lg, rg, basis3, left, right, basis3, basis4)


def fast(rows, cols, left, right, basis, block):
    acc, lct, rc, lg, rg = gather_product(left, right, basis, block, rows, cols)
    return finish(acc, lct, rc, lg, rg, left, right, basis, rows, cols)


def plain(left, right, basis, block):
    ml = left.shape[0]
    mr = right.shape[0]
    whole_left = lax.all_gather(left, "col", axis=0, tiled=True)
    whole_right = lax.all_gather(right, "row", axis=0, tiled=True)
    bl = lax.dynamic_slice_in_dim(basis, lax.axis_index("col") * ml, ml, 0)
    br = lax.dynamic_slice_in_dim(basis, lax.axis_index("row") * mr, mr, 0)
    lc = dot(basis, whole_left, ((0,), (0,)))
    rc = dot(basis, whole_right, ((0,), (0,)))
    updated = block + dot(whole_left, whole_right, ((0,), (0,))) - dot(lc, rc, ((0,), (0,)))
    left_reduced = left - dot(bl, lc, ((1,), (0,)))
    right_reduced = right - dot(br, rc, ((1,), (0,)))
    return updated, left_reduced, right_reduced


def solution(mesh):
    rows, cols = mesh.shape["row"], mesh.shape["col"]
    local = functools.partial(fast, rows, cols) if (rows, cols) == (4, 8) else plain
    in_specs = (P("col", "row"), P("row", "col"), P(), P("row", "col"))
    out_specs = (P("row", "col"), P("col", "row"), P("row", "col"))
    return jax.shard_map(
        local, mesh=mesh, in_specs=in_specs, out_specs=out_specs, check_vma=False
    )
```

```python
import functools

import jax
import jax.numpy as jnp
from jax import lax
from jax.experimental import pallas as pl
from jax.experimental.pallas import tpu as pltpu
from jax.sharding import PartitionSpec as P

COMM = True
COMPUTE = True
STEPS = 32
GROUP = 2
CUT1 = 0
CUT2 = 3
CUT3 = 5

MESH = pl.DeviceIdType.MESH
F32 = jnp.float32
BF16 = jnp.bfloat16


def split(x):
    hi = x.astype(BF16)
    lo = (x - hi.astype(F32)).astype(BF16)
    return hi, lo


def kernel(
    steps, left, right, basis, block, acc_o, lg, rg,
    acc, lbuf, rbuf, qv, lt3, r3, ltail, rtail,
    s_own, s_relay, s_fwd, s_right, r_left, r_fwd, r_right, ld_sem, misc, tail_sem, out_sem,
):
    r = lax.axis_index("row")
    c = lax.axis_index("col")
    z = c // 2
    k = c % 2
    sib = c + 1 - 2 * k
    rx = r + 1 - 2 * (r % 2)
    ry = (r + 2) % 4
    lr = lbuf.shape[3]
    nl = left.shape[1]
    nr = right.shape[2]
    ka = basis.shape[2]

    def remote(src, dst, ss, rs, row, col):
        return pltpu.make_async_remote_copy(
            src_ref=src, dst_ref=dst, send_sem=ss, recv_sem=rs,
            device_id={"row": row, "col": col}, device_id_type=MESH,
        )

    def mine(s):
        return left.at[pl.ds(pl.multiple_of(s * lr, lr), lr), :]

    def own_up(s):
        return remote(mine(s), lg.at[s, c], s_own.at[s, 0], r_left.at[s, z], r, c + 2)

    def own_dn(s):
        return remote(mine(s), lg.at[s, c], s_own.at[s, 1], r_left.at[s, z], r, c - 2)

    def own_far(s):
        far = 6 + k - 6 * (z // 3)
        return remote(mine(s), lg.at[s, c], s_own.at[s, 2], r_left.at[s, z], r, far)

    def relay_up(s):
        return remote(lg.at[s, c - 2], lg.at[s, c - 2], s_relay.at[s, 0], r_left.at[s, z - 1], r, c + 2)

    def relay_dn(s):
        return remote(lg.at[s, c + 2], lg.at[s, c + 2], s_relay.at[s, 1], r_left.at[s, z + 1], r, c - 2)

    def fwd_own(s):
        return remote(mine(s), lg.at[s, c], s_fwd.at[s, z], r_fwd.at[s, z], r, sib)

    def fwd(s, o):
        at = lg.at[s, 2 * o + k]
        return remote(at, at, s_fwd.at[s, o], r_fwd.at[s, o], r, sib)

    def arrived(s, o):
        at = lg.at[s, 2 * o + k]
        return remote(at, at, s_fwd.at[s, o], r_left.at[s, o], r, sib)

    def own_r(s, i, row):
        src = right.at[:, pl.ds(pl.multiple_of(s * lr, lr), lr), :]
        return remote(src, rg.at[s, r], s_right.at[s, i], r_right.at[s, i], row, c)

    def relay_r(s, i, owner, row):
        at = rg.at[s, owner, i]
        return remote(at, at, s_right.at[s, 2 + i], r_right.at[s, 2 + i], row, c)

    def start_own(s):
        own_r(s, 0, rx).start()
        own_r(s, 1, ry).start()

        @pl.when(z < 3)
        def _():
            own_up(s).start()

        @pl.when(z > 0)
        def _():
            own_dn(s).start()

        @pl.when(z % 3 == 0)
        def _():
            own_far(s).start()

        fwd_own(s).start()

    def stage1(s):
        own_r(s, 0, rx).wait_recv()
        relay_r(s, 0, rx, ry).start()
        own_r(s, 1, ry).wait_recv()
        relay_r(s, 1, ry, rx).start()

        @pl.when(z > 0)
        def _():
            arrived(s, z - 1).wait_recv()

            @pl.when(z < 3)
            def _():
                relay_up(s).start()

            fwd(s, z - 1).start()

        @pl.when(z < 3)
        def _():
            arrived(s, z + 1).wait_recv()

            @pl.when(z > 0)
            def _():
                relay_dn(s).start()

            fwd(s, z + 1).start()

    def stage2(s):
        far = (z + 2) % 4
        arrived(s, far).wait_recv()
        fwd(s, far).start()

        @pl.when(z % 3 == 0)
        def _():
            end = 3 - z
            arrived(s, end).wait_recv()
            fwd(s, end).start()

        relay_r(s, 0, rx, ry).wait_recv()
        relay_r(s, 1, ry, rx).wait_recv()

    def stage3(s):
        @pl.loop(0, 4)
        def _(o):
            at = lg.at[s, 2 * o + 1 - k]
            remote(at, at, s_fwd.at[s, o], r_fwd.at[s, o], r, sib).wait_recv()

    def load(s):
        slot = (s // GROUP) % 2
        i = s % GROUP
        pltpu.make_async_copy(mine(s), lbuf.at[slot, i, c], ld_sem.at[0, slot, i]).start()
        src = right.at[:, pl.ds(pl.multiple_of(s * lr, lr), lr), :]
        pltpu.make_async_copy(src, rbuf.at[slot, i, r], ld_sem.at[1, slot, i]).start()

        @pl.loop(1, 8)
        def _(d):
            o = (c + d) % 8
            pltpu.make_async_copy(lg.at[s, o], lbuf.at[slot, i, o], ld_sem.at[0, slot, i]).start()

        @pl.loop(1, 4)
        def _(d):
            o = (r + d) % 4
            pltpu.make_async_copy(rg.at[s, o], rbuf.at[slot, i, o], ld_sem.at[1, slot, i]).start()

    def loaded(s):
        slot = (s // GROUP) % 2
        i = s % GROUP
        pltpu.make_async_copy(lg.at[s], lbuf.at[slot, i], ld_sem.at[0, slot, i]).wait()
        pltpu.make_async_copy(rg.at[s], rbuf.at[slot, i], ld_sem.at[1, slot, i]).wait()

    depth = GROUP * 8 * lr

    def put_left(x, at):
        hi, lo = split(x.T)
        lt3[pl.ds(at, 256), 0:depth] = hi
        lt3[pl.ds(at, 256), depth : 2 * depth] = lo
        lt3[pl.ds(at, 256), 2 * depth : 3 * depth] = hi

    def put_right(x, at):
        hi, lo = split(x)
        r3[0:depth, pl.ds(at, 256)] = hi
        r3[depth : 2 * depth, pl.ds(at, 256)] = hi
        r3[2 * depth : 3 * depth, pl.ds(at, 256)] = lo

    def prepare(j):
        slot = j % 2

        @pl.loop(0, nl // 256)
        def _(b):
            at = pl.multiple_of(b * 256, 256)
            put_left(lbuf[slot, :, :, :, pl.ds(at, 256)].reshape(depth, 256), at)

        @pl.loop(0, nr // 256)
        def _(b):
            at = pl.multiple_of(b * 256, 256)
            put_right(rbuf[slot, :, :, :, :, pl.ds(at, 256)].reshape(depth, 256), at)

        q = qv[:, pl.ds(pl.multiple_of(j * GROUP * lr, GROUP * lr), GROUP * lr), :]
        q = jnp.concatenate(
            [q[:, i * lr : (i + 1) * lr].reshape(8 * lr, ka) for i in range(GROUP)], axis=0
        )
        put_left(q, nl)
        put_right(q, nr)

    tiles_n = (nr + ka) // 256

    def columns(n):
        return pl.ds(pl.multiple_of((n + tiles_n - 1) % tiles_n * 256, 256), 256)

    def out_tile(n):
        cols = columns(n)
        return pltpu.make_async_copy(acc.at[:, cols], acc_o.at[:, cols], out_sem.at[n])

    if True:
        barrier = pltpu.get_barrier_semaphore()
        za = (z + 1) % 4
        zb = (z + 3) % 4
        for row, col in ((rx, c), (ry, c), (r, sib), (r, 2 * za + k), (r, 2 * zb + k)):
            pl.semaphore_signal(barrier, inc=1, device_id={"row": row, "col": col}, device_id_type=MESH)
        pl.semaphore_wait(barrier, 5)
    if COMM:
        for s in range(GROUP):
            start_own(s)

    fill = pltpu.make_async_copy(block, acc.at[0:nl, 0:nr], misc.at[0])
    fill.start()
    qfill = pltpu.make_async_copy(basis, qv, misc.at[1])
    qfill.start()
    acc[nl:, :] = jnp.zeros((ka, nr + ka), F32)
    acc[0:nl, nr:] = jnp.zeros((nl, ka), F32)

    first = steps - GROUP
    tail_in = []
    tail_out = []
    for i in range(GROUP):
        at = pl.ds((first + i) * lr, lr)
        tail_in += [
            pltpu.make_async_copy(left.at[at, :], ltail.at[i], tail_sem.at[0, i]),
            pltpu.make_async_copy(right.at[:, at, :], rtail.at[i], tail_sem.at[1, i]),
        ]
        tail_out += [
            pltpu.make_async_copy(ltail.at[i], lg.at[first + i, c], tail_sem.at[2, i]),
            pltpu.make_async_copy(rtail.at[i], rg.at[first + i, r], tail_sem.at[3, i]),
        ]
    for copy in tail_in:
        copy.start()

    end = steps - GROUP

    @pl.loop(0, steps // GROUP)
    def _(h):
        t = h * GROUP

        if COMM:
            stage1(t)

            @pl.when(t > 0)
            def _():
                stage3(t - 2)
        if COMPUTE:
            @pl.when(t > 0)
            def _():
                load(t - 2)
        if COMM:
            @pl.when(t > 0)
            def _():
                stage2(t - 1)
                stage3(t - 1)
        if COMPUTE:
            @pl.when(t > 0)
            def _():
                load(t - 1)
        if COMM:
            @pl.when(t < end)
            def _():
                start_own(t + 2)

        if COMPUTE:
            @pl.when(t == GROUP)
            def _():
                fill.wait()
                qfill.wait()
                for copy in tail_in:
                    copy.wait()
                for copy in tail_out:
                    copy.start()

            @pl.when(t > 0)
            def _():
                loaded(t - 2)
                loaded(t - 1)
                prepare(h - 1)

        @pl.loop(0, tiles_n)
        def _(n):
            if COMPUTE:
                @pl.when(t > 0)
                def _():
                    cols = columns(n)
                    acc[:, cols] += jnp.dot(lt3[...], r3[:, cols], preferred_element_type=F32)

                @pl.when(t == end)
                def _():
                    out_tile(n).start()

            if COMM:
                @pl.when(n == CUT1)
                def _():
                    stage1(t + 1)

                @pl.when(n == CUT2)
                def _():
                    stage2(t)

                    @pl.when(t < end)
                    def _():
                        start_own(t + 3)

                @pl.when((n == CUT3) & (t == end))
                def _():
                    stage2(t + 1)

    if COMM:
        for s in range(end, steps):
            stage3(s)

    if COMM:
        @pl.loop(0, steps)
        def _(s):
            own_r(s, 0, rx).wait_send()
            own_r(s, 1, ry).wait_send()
            relay_r(s, 0, rx, ry).wait_send()
            relay_r(s, 1, ry, rx).wait_send()
            fwd_own(s).wait_send()

            @pl.loop(1, 4)
            def _(d):
                fwd(s, (z + d) % 4).wait_send()

            @pl.when(z < 3)
            def _():
                own_up(s).wait_send()

            @pl.when(z > 0)
            def _():
                own_dn(s).wait_send()

            @pl.when(z % 3 == 0)
            def _():
                own_far(s).wait_send()

            @pl.when((z > 0) & (z < 3))
            def _():
                relay_up(s).wait_send()
                relay_dn(s).wait_send()

    if not COMPUTE:
        for copy in tail_in + [fill, qfill]:
            copy.wait()
    if COMPUTE:
        for copy in tail_out:
            copy.wait()

        @pl.loop(0, tiles_n)
        def _(n):
            out_tile(n).wait()


def gather_product(left, right, basis, block, rows, cols):
    steps = STEPS
    ml, nl = left.shape
    mr, nr = right.shape
    ka = basis.shape[1]
    lr = ml // steps
    right3 = right.reshape(cols // rows, ml, nr)
    basis3 = basis.reshape(cols, ml, ka)
    any_spec = pl.BlockSpec(memory_space=pl.ANY)
    dma = pltpu.SemaphoreType.DMA
    return pl.pallas_call(
        functools.partial(kernel, steps),
        out_shape=(
            jax.ShapeDtypeStruct((nl + ka, nr + ka), F32),
            jax.ShapeDtypeStruct((steps, cols, lr, nl), F32),
            jax.ShapeDtypeStruct((steps, rows, cols // rows, lr, nr), F32),
        ),
        in_specs=[any_spec] * 4,
        out_specs=[any_spec] * 3,
        scratch_shapes=[
            pltpu.VMEM((nl + ka, nr + ka), F32),
            pltpu.VMEM((2, GROUP, cols, lr, nl), F32),
            pltpu.VMEM((2, GROUP, rows, cols // rows, lr, nr), F32),
            pltpu.VMEM((cols, ml, ka), F32),
            pltpu.VMEM((nl + ka, 3 * GROUP * cols * lr), BF16),
            pltpu.VMEM((3 * GROUP * cols * lr, nr + ka), BF16),
            pltpu.VMEM((GROUP, lr, nl), F32),
            pltpu.VMEM((GROUP, cols // rows, lr, nr), F32),
            dma((steps, 3)),
            dma((steps, 2)),
            dma((steps, 4)),
            dma((steps, 4)),
            dma((steps, 4)),
            dma((steps, 4)),
            dma((steps, 4)),
            dma((2, 2, GROUP)),
            dma((2,)),
            dma((4, GROUP)),
            dma(((nr + ka) // 256,)),
        ],
        compiler_params=pltpu.CompilerParams(
            collective_id=0, has_side_effects=True, vmem_limit_bytes=64000 * 1024
        ),
        name="gather_product",
    )(left, right3, basis3, block)


def dot(a, b, dims):
    return lax.dot_general(
        a, b, (dims, ((), ())), precision=lax.Precision.HIGH, preferred_element_type=F32
    )


def finish_kernel(
    acc, lct, rc, lg, rg, qt, left, right, ql, qr, out, left_o, right_o,
    lt3, qth, qtl, qls, qrs,
):
    n = pl.program_id(0)
    group, parts, lr = lg.shape[0], lg.shape[1], lg.shape[2]
    depth = group * parts * lr
    nl, ka = lct.shape
    mm = functools.partial(jnp.dot, preferred_element_type=F32)

    def nt(a, b):
        return lax.dot_general(a, b, (((1,), (1,)), ((), ())), preferred_element_type=F32)

    @pl.when(n == 0)
    def _():
        q = jnp.concatenate(
            [qt[:, i * lr : (i + 1) * lr].reshape(parts * lr, ka) for i in range(group)], axis=0
        )
        qh, qlo = split(q)
        hi, lo = split(q.T)
        qth[...] = hi
        qtl[...] = lo
        hi, lo = split(ql[0])
        qls[:, 0:ka] = hi
        qls[:, ka:] = lo
        hi, lo = split(qr[0])
        qrs[:, 0:ka] = hi
        qrs[:, ka:] = lo

        @pl.loop(0, nl // 256)
        def _(b):
            at = pl.ds(pl.multiple_of(b * 256, 256), 256)
            hi, lo = split(lg[:, :, :, at].reshape(depth, 256).T)
            lt3[at, 0:depth] = hi
            lt3[at, depth : 2 * depth] = lo
            lt3[at, 2 * depth : 3 * depth] = hi
            coef = lct[at, :] + (mm(hi, qh) + mm(lo, qh) + mm(hi, qlo))
            hi, lo = split(-coef)
            base = 3 * depth
            lt3[at, base : base + ka] = hi
            lt3[at, base + ka : base + 2 * ka] = lo
            lt3[at, base + 2 * ka :] = hi

    y = rg[...].reshape(depth, rg.shape[-1])
    yh, yl = split(y)
    coef = rc[...] + (mm(qth[...], yh) + mm(qtl[...], yh) + mm(qth[...], yl))
    ch, cl = split(coef)
    r3 = jnp.concatenate([yh, yh, yl, ch, ch, cl], axis=0)
    out[...] = acc[...] + mm(lt3[...], r3)
    qh, qlo = qrs[:, 0:ka], qrs[:, ka:]
    right_o[...] = right[...] - (mm(qh, ch) + mm(qlo, ch) + mm(qh, cl))
    at = pl.ds(pl.multiple_of(n * 256, 256), 256)
    base = 3 * depth
    lh = lt3[at, base : base + ka]
    ll = lt3[at, base + ka : base + 2 * ka]
    qh, qlo = qls[:, 0:ka], qls[:, ka:]
    left_o[...] = left[...] + (nt(qh, lh) + nt(qlo, lh) + nt(qh, ll))


def finish(acc, lg, rg, left, right, basis, rows, cols):
    ml, nl = left.shape
    mr, nr = right.shape
    ka = basis.shape[1]
    steps, _, lr, _ = lg.shape
    last = steps // GROUP - 1
    depth = GROUP * cols * lr
    basis3 = basis.reshape(cols, ml, ka)
    basis4 = basis.reshape(rows, mr, ka)
    tile = lambda height: pl.BlockSpec((height, 256), lambda n: (0, n))
    once = lambda shape, index: pl.BlockSpec(shape, lambda n: index, pipeline_mode=pl.Buffered(1))
    return pl.pallas_call(
        finish_kernel,
        grid=(nr // 256,),
        out_shape=(
            jax.ShapeDtypeStruct((nl, nr), F32),
            jax.ShapeDtypeStruct((ml, nl), F32),
            jax.ShapeDtypeStruct((mr, nr), F32),
        ),
        in_specs=[
            tile(nl),
            once((nl, ka), (0, nr // ka)),
            pl.BlockSpec((ka, 256), lambda n: (nl // ka, n)),
            once((GROUP, cols, lr, nl), (last, 0, 0, 0)),
            pl.BlockSpec((GROUP, rows, cols // rows, lr, 256), lambda n: (last, 0, 0, 0, n)),
            once((cols, GROUP * lr, ka), (0, last, 0)),
            tile(ml),
            tile(mr),
            pl.BlockSpec((1, ml, ka), lambda n: (lax.axis_index("col"), 0, 0), pipeline_mode=pl.Buffered(1)),
            pl.BlockSpec((1, mr, ka), lambda n: (lax.axis_index("row"), 0, 0), pipeline_mode=pl.Buffered(1)),
        ],
        out_specs=[tile(nl), tile(ml), tile(mr)],
        scratch_shapes=[
            pltpu.VMEM((nl, 3 * depth + 3 * ka), BF16),
            pltpu.VMEM((ka, depth), BF16),
            pltpu.VMEM((ka, depth), BF16),
            pltpu.VMEM((ml, 2 * ka), BF16),
            pltpu.VMEM((mr, 2 * ka), BF16),
        ],
        compiler_params=pltpu.CompilerParams(
            dimension_semantics=("arbitrary",), vmem_limit_bytes=60000 * 1024
        ),
        name="finish",
    )(acc, acc, acc, lg, rg, basis3, left, right, basis3, basis4)


def fast(rows, cols, left, right, basis, block):
    acc, lg, rg = gather_product(left, right, basis, block, rows, cols)
    return finish(acc, lg, rg, left, right, basis, rows, cols)


def plain(left, right, basis, block):
    ml = left.shape[0]
    mr = right.shape[0]
    whole_left = lax.all_gather(left, "col", axis=0, tiled=True)
    whole_right = lax.all_gather(right, "row", axis=0, tiled=True)
    bl = lax.dynamic_slice_in_dim(basis, lax.axis_index("col") * ml, ml, 0)
    br = lax.dynamic_slice_in_dim(basis, lax.axis_index("row") * mr, mr, 0)
    lc = dot(basis, whole_left, ((0,), (0,)))
    rc = dot(basis, whole_right, ((0,), (0,)))
    updated = block + dot(whole_left, whole_right, ((0,), (0,))) - dot(lc, rc, ((0,), (0,)))
    left_reduced = left - dot(bl, lc, ((1,), (0,)))
    right_reduced = right - dot(br, rc, ((1,), (0,)))
    return updated, left_reduced, right_reduced


def solution(mesh):
    rows, cols = mesh.shape["row"], mesh.shape["col"]
    local = functools.partial(fast, rows, cols) if (rows, cols) == (4, 8) else plain
    in_specs = (P("col", "row"), P("row", "col"), P(), P("row", "col"))
    out_specs = (P("row", "col"), P("col", "row"), P("row", "col"))
    return jax.shard_map(
        local, mesh=mesh, in_specs=in_specs, out_specs=out_specs, check_vma=False
    )
```

```python
import functools

import jax
import jax.numpy as jnp
from jax import lax
from jax.experimental import pallas as pl
from jax.experimental.pallas import tpu as pltpu
from jax.sharding import PartitionSpec as P

COMM = True
COMPUTE = True
STEPS = 32
GROUP = 2
CUT1 = 0
CUT2 = 3
CUT3 = 5

MESH = pl.DeviceIdType.MESH
F32 = jnp.float32
BF16 = jnp.bfloat16


def split(x):
    hi = x.astype(BF16)
    lo = (x - hi.astype(F32)).astype(BF16)
    return hi, lo


def kernel(
    steps, left, right, basis, block, acc_o, lg, rg,
    acc, lbuf, rbuf, qv, lt3, r3, ltail, rtail,
    s_own, s_relay, s_fwd, s_right, r_left, r_fwd, r_right, ld_sem, misc, tail_sem, out_sem,
):
    r = lax.axis_index("row")
    c = lax.axis_index("col")
    z = c // 2
    k = c % 2
    sib = c + 1 - 2 * k
    rx = r + 1 - 2 * (r % 2)
    ry = (r + 2) % 4
    lr = lbuf.shape[3]
    nl = left.shape[1]
    nr = right.shape[2]
    ka = basis.shape[2]

    def remote(src, dst, ss, rs, row, col):
        return pltpu.make_async_remote_copy(
            src_ref=src, dst_ref=dst, send_sem=ss, recv_sem=rs,
            device_id={"row": row, "col": col}, device_id_type=MESH,
        )

    def mine(s):
        return left.at[pl.ds(pl.multiple_of(s * lr, lr), lr), :]

    def own_up(s):
        return remote(mine(s), lg.at[s, c], s_own.at[s, 0], r_left.at[s, z], r, c + 2)

    def own_dn(s):
        return remote(mine(s), lg.at[s, c], s_own.at[s, 1], r_left.at[s, z], r, c - 2)

    def own_far(s):
        far = 6 + k - 6 * (z // 3)
        return remote(mine(s), lg.at[s, c], s_own.at[s, 2], r_left.at[s, z], r, far)

    def relay_up(s):
        return remote(lg.at[s, c - 2], lg.at[s, c - 2], s_relay.at[s, 0], r_left.at[s, z - 1], r, c + 2)

    def relay_dn(s):
        return remote(lg.at[s, c + 2], lg.at[s, c + 2], s_relay.at[s, 1], r_left.at[s, z + 1], r, c - 2)

    def fwd_own(s):
        return remote(mine(s), lg.at[s, c], s_fwd.at[s, z], r_fwd.at[s, z], r, sib)

    def fwd(s, o):
        at = lg.at[s, 2 * o + k]
        return remote(at, at, s_fwd.at[s, o], r_fwd.at[s, o], r, sib)

    def arrived(s, o):
        at = lg.at[s, 2 * o + k]
        return remote(at, at, s_fwd.at[s, o], r_left.at[s, o], r, sib)

    def own_r(s, i, row):
        src = right.at[:, pl.ds(pl.multiple_of(s * lr, lr), lr), :]
        return remote(src, rg.at[s, r], s_right.at[s, i], r_right.at[s, i], row, c)

    def relay_r(s, i, owner, row):
        at = rg.at[s, owner, i]
        return remote(at, at, s_right.at[s, 2 + i], r_right.at[s, 2 + i], row, c)

    def start_own(s):
        own_r(s, 0, rx).start()
        own_r(s, 1, ry).start()

        @pl.when(z < 3)
        def _():
            own_up(s).start()

        @pl.when(z > 0)
        def _():
            own_dn(s).start()

        @pl.when(z % 3 == 0)
        def _():
            own_far(s).start()

        fwd_own(s).start()

    def stage1(s):
        own_r(s, 0, rx).wait_recv()
        relay_r(s, 0, rx, ry).start()
        own_r(s, 1, ry).wait_recv()
        relay_r(s, 1, ry, rx).start()

        @pl.when(z > 0)
        def _():
            arrived(s, z - 1).wait_recv()

            @pl.when(z < 3)
            def _():
                relay_up(s).start()

            fwd(s, z - 1).start()

        @pl.when(z < 3)
        def _():
            arrived(s, z + 1).wait_recv()

            @pl.when(z > 0)
            def _():
                relay_dn(s).start()

            fwd(s, z + 1).start()

    def stage2(s):
        far = (z + 2) % 4
        arrived(s, far).wait_recv()
        fwd(s, far).start()

        @pl.when(z % 3 == 0)
        def _():
            end = 3 - z
            arrived(s, end).wait_recv()
            fwd(s, end).start()

        relay_r(s, 0, rx, ry).wait_recv()
        relay_r(s, 1, ry, rx).wait_recv()

    def stage3(s):
        @pl.loop(0, 4)
        def _(o):
            at = lg.at[s, 2 * o + 1 - k]
            remote(at, at, s_fwd.at[s, o], r_fwd.at[s, o], r, sib).wait_recv()

    def load(s):
        slot = (s // GROUP) % 2
        i = s % GROUP
        pltpu.make_async_copy(mine(s), lbuf.at[slot, i, c], ld_sem.at[0, slot, i]).start()
        src = right.at[:, pl.ds(pl.multiple_of(s * lr, lr), lr), :]
        pltpu.make_async_copy(src, rbuf.at[slot, i, r], ld_sem.at[1, slot, i]).start()

        @pl.loop(1, 8)
        def _(d):
            o = (c + d) % 8
            pltpu.make_async_copy(lg.at[s, o], lbuf.at[slot, i, o], ld_sem.at[0, slot, i]).start()

        @pl.loop(1, 4)
        def _(d):
            o = (r + d) % 4
            pltpu.make_async_copy(rg.at[s, o], rbuf.at[slot, i, o], ld_sem.at[1, slot, i]).start()

    def loaded(s):
        slot = (s // GROUP) % 2
        i = s % GROUP
        pltpu.make_async_copy(lg.at[s], lbuf.at[slot, i], ld_sem.at[0, slot, i]).wait()
        pltpu.make_async_copy(rg.at[s], rbuf.at[slot, i], ld_sem.at[1, slot, i]).wait()

    depth = GROUP * 8 * lr

    def put_left(x, at):
        hi, lo = split(x.T)
        lt3[pl.ds(at, 256), 0:depth] = hi
        lt3[pl.ds(at, 256), depth : 2 * depth] = lo
        lt3[pl.ds(at, 256), 2 * depth : 3 * depth] = hi

    def put_right(x, at):
        hi, lo = split(x)
        r3[0:depth, pl.ds(at, 256)] = hi
        r3[depth : 2 * depth, pl.ds(at, 256)] = hi
        r3[2 * depth : 3 * depth, pl.ds(at, 256)] = lo

    def prepare(j):
        slot = j % 2

        @pl.loop(0, nl // 256)
        def _(b):
            at = pl.multiple_of(b * 256, 256)
            put_left(lbuf[slot, :, :, :, pl.ds(at, 256)].reshape(depth, 256), at)

        @pl.loop(0, nr // 256)
        def _(b):
            at = pl.multiple_of(b * 256, 256)
            put_right(rbuf[slot, :, :, :, :, pl.ds(at, 256)].reshape(depth, 256), at)

        q = qv[:, pl.ds(pl.multiple_of(j * GROUP * lr, GROUP * lr), GROUP * lr), :]
        q = jnp.concatenate(
            [q[:, i * lr : (i + 1) * lr].reshape(8 * lr, ka) for i in range(GROUP)], axis=0
        )
        put_left(q, nl)
        put_right(q, nr)

    tiles_n = (nr + ka) // 256

    def columns(n):
        return pl.ds(pl.multiple_of((n + tiles_n - 1) % tiles_n * 256, 256), 256)

    def out_tile(n):
        cols = columns(n)
        return pltpu.make_async_copy(acc.at[:, cols], acc_o.at[:, cols], out_sem.at[n])

    if True:
        barrier = pltpu.get_barrier_semaphore()
        za = (z + 1) % 4
        zb = (z + 3) % 4
        for row, col in ((rx, c), (ry, c), (r, sib), (r, 2 * za + k), (r, 2 * zb + k)):
            pl.semaphore_signal(barrier, inc=1, device_id={"row": row, "col": col}, device_id_type=MESH)
        pl.semaphore_wait(barrier, 5)
    if COMM:
        for s in range(GROUP):
            start_own(s)

    fill = pltpu.make_async_copy(block, acc.at[0:nl, 0:nr], misc.at[0])
    fill.start()
    qfill = pltpu.make_async_copy(basis, qv, misc.at[1])
    qfill.start()
    acc[nl:, :] = jnp.zeros((ka, nr + ka), F32)
    acc[0:nl, nr:] = jnp.zeros((nl, ka), F32)

    first = steps - GROUP
    tail_in = []
    tail_out = []
    for i in range(GROUP):
        at = pl.ds((first + i) * lr, lr)
        tail_in += [
            pltpu.make_async_copy(left.at[at, :], ltail.at[i], tail_sem.at[0, i]),
            pltpu.make_async_copy(right.at[:, at, :], rtail.at[i], tail_sem.at[1, i]),
        ]
        tail_out += [
            pltpu.make_async_copy(ltail.at[i], lg.at[first + i, c], tail_sem.at[2, i]),
            pltpu.make_async_copy(rtail.at[i], rg.at[first + i, r], tail_sem.at[3, i]),
        ]
    for copy in tail_in:
        copy.start()

    end = steps - GROUP

    @pl.loop(0, steps // GROUP)
    def _(h):
        t = h * GROUP

        if COMM:
            stage1(t)

            @pl.when(t > 0)
            def _():
                stage3(t - 2)
        if COMPUTE:
            @pl.when(t > 0)
            def _():
                load(t - 2)
        if COMM:
            @pl.when(t > 0)
            def _():
                stage2(t - 1)
                stage3(t - 1)
        if COMPUTE:
            @pl.when(t > 0)
            def _():
                load(t - 1)
        if COMM:
            @pl.when(t < end)
            def _():
                start_own(t + 2)

        if COMPUTE:
            @pl.when(t == GROUP)
            def _():
                fill.wait()
                qfill.wait()
                for copy in tail_in:
                    copy.wait()
                for copy in tail_out:
                    copy.start()

            @pl.when(t > 0)
            def _():
                loaded(t - 2)
                loaded(t - 1)
                prepare(h - 1)

        @pl.loop(0, tiles_n)
        def _(n):
            if COMPUTE:
                @pl.when(t > 0)
                def _():
                    cols = columns(n)
                    acc[:, cols] += jnp.dot(lt3[...], r3[:, cols], preferred_element_type=F32)

                @pl.when(t == end)
                def _():
                    out_tile(n).start()

            if COMM:
                @pl.when(n == CUT1)
                def _():
                    stage1(t + 1)

                @pl.when(n == CUT2)
                def _():
                    stage2(t)

                    @pl.when(t < end)
                    def _():
                        start_own(t + 3)

                @pl.when((n == CUT3) & (t == end))
                def _():
                    stage2(t + 1)

    if COMM:
        for s in range(end, steps):
            stage3(s)

    if COMM:
        @pl.loop(0, steps)
        def _(s):
            own_r(s, 0, rx).wait_send()
            own_r(s, 1, ry).wait_send()
            relay_r(s, 0, rx, ry).wait_send()
            relay_r(s, 1, ry, rx).wait_send()
            fwd_own(s).wait_send()

            @pl.loop(1, 4)
            def _(d):
                fwd(s, (z + d) % 4).wait_send()

            @pl.when(z < 3)
            def _():
                own_up(s).wait_send()

            @pl.when(z > 0)
            def _():
                own_dn(s).wait_send()

            @pl.when(z % 3 == 0)
            def _():
                own_far(s).wait_send()

            @pl.when((z > 0) & (z < 3))
            def _():
                relay_up(s).wait_send()
                relay_dn(s).wait_send()

    if not COMPUTE:
        for copy in tail_in + [fill, qfill]:
            copy.wait()
    if COMPUTE:
        for copy in tail_out:
            copy.wait()

        @pl.loop(0, tiles_n)
        def _(n):
            out_tile(n).wait()


def gather_product(left, right, basis, block, rows, cols):
    steps = STEPS
    ml, nl = left.shape
    mr, nr = right.shape
    ka = basis.shape[1]
    lr = ml // steps
    right3 = right.reshape(cols // rows, ml, nr)
    basis3 = basis.reshape(cols, ml, ka)
    any_spec = pl.BlockSpec(memory_space=pl.ANY)
    dma = pltpu.SemaphoreType.DMA
    return pl.pallas_call(
        functools.partial(kernel, steps),
        out_shape=(
            jax.ShapeDtypeStruct((nl + ka, nr + ka), F32),
            jax.ShapeDtypeStruct((steps, cols, lr, nl), F32),
            jax.ShapeDtypeStruct((steps, rows, cols // rows, lr, nr), F32),
        ),
        in_specs=[any_spec] * 4,
        out_specs=[any_spec] * 3,
        scratch_shapes=[
            pltpu.VMEM((nl + ka, nr + ka), F32),
            pltpu.VMEM((2, GROUP, cols, lr, nl), F32),
            pltpu.VMEM((2, GROUP, rows, cols // rows, lr, nr), F32),
            pltpu.VMEM((cols, ml, ka), F32),
            pltpu.VMEM((nl + ka, 3 * GROUP * cols * lr), BF16),
            pltpu.VMEM((3 * GROUP * cols * lr, nr + ka), BF16),
            pltpu.VMEM((GROUP, lr, nl), F32),
            pltpu.VMEM((GROUP, cols // rows, lr, nr), F32),
            dma((steps, 3)),
            dma((steps, 2)),
            dma((steps, 4)),
            dma((steps, 4)),
            dma((steps, 4)),
            dma((steps, 4)),
            dma((steps, 4)),
            dma((2, 2, GROUP)),
            dma((2,)),
            dma((4, GROUP)),
            dma(((nr + ka) // 256,)),
        ],
        compiler_params=pltpu.CompilerParams(
            collective_id=0, has_side_effects=True, vmem_limit_bytes=64000 * 1024
        ),
        name="gather_product",
    )(left, right3, basis3, block)


def dot(a, b, dims):
    return lax.dot_general(
        a, b, (dims, ((), ())), precision=lax.Precision.HIGH, preferred_element_type=F32
    )


def finish_kernel(
    acc, lg, rg, qt, left, right, ql, qr, out, left_o, right_o,
    lt3, qth, qtl, qls, qrs, accv, lctv, lgv, rgv, lv, rv, sem, sem_l,
):
    n = pl.program_id(0)
    group, parts, lr = lgv.shape[0], lgv.shape[1], lgv.shape[2]
    depth = group * parts * lr
    ka = qth.shape[0]
    nl = lgv.shape[3]
    nr = rv.shape[1]
    last = lg.shape[0] // group - 1
    mm = functools.partial(jnp.dot, preferred_element_type=F32)

    def nt(a, b):
        return lax.dot_general(a, b, (((1,), (1,)), ((), ())), preferred_element_type=F32)

    def span(i):
        return pl.ds(pl.multiple_of(i * 256, 256), 256)

    tail = pl.ds(last * group, group)

    def left_in(b):
        at = span(b)
        return (
            pltpu.make_async_copy(acc.at[at, nr:], lctv.at[at, :], sem_l.at[0, b]),
            pltpu.make_async_copy(lg.at[tail, :, :, at], lgv.at[:, :, :, at], sem_l.at[1, b]),
        )

    def tile_in(i):
        at = span(i)
        return (
            pltpu.make_async_copy(rg.at[tail, :, :, :, at], rgv.at[:, :, :, :, at], sem.at[0, i]),
            pltpu.make_async_copy(acc.at[:, at], accv.at[:, at], sem.at[1, i]),
            pltpu.make_async_copy(right.at[:, at], rv.at[:, at], sem.at[2, i]),
            pltpu.make_async_copy(left.at[:, at], lv.at[:, at], sem.at[3, i]),
        )

    @pl.when(n == 0)
    def _():
        @pl.loop(0, nl // 256)
        def _(b):
            for copy in left_in(b):
                copy.start()

        @pl.loop(0, nr // 256)
        def _(i):
            for copy in tile_in(i):
                copy.start()

        q = jnp.concatenate(
            [qt[:, i * lr : (i + 1) * lr].reshape(parts * lr, ka) for i in range(group)], axis=0
        )
        qh, qlo = split(q)
        hi, lo = split(q.T)
        qth[...] = hi
        qtl[...] = lo
        hi, lo = split(ql[0])
        qls[:, 0:ka] = hi
        qls[:, ka:] = lo
        hi, lo = split(qr[0])
        qrs[:, 0:ka] = hi
        qrs[:, ka:] = lo

        @pl.loop(0, nl // 256)
        def _(b):
            for copy in left_in(b):
                copy.wait()
            at = span(b)
            hi, lo = split(lgv[:, :, :, at].reshape(depth, 256).T)
            lt3[at, 0:depth] = hi
            lt3[at, depth : 2 * depth] = lo
            lt3[at, 2 * depth : 3 * depth] = hi
            coef = lctv[at, :] + (mm(hi, qh) + mm(lo, qh) + mm(hi, qlo))
            hi, lo = split(-coef)
            base = 3 * depth
            lt3[at, base : base + ka] = hi
            lt3[at, base + ka : base + 2 * ka] = lo
            lt3[at, base + 2 * ka :] = hi

    for copy in tile_in(n):
        copy.wait()
    at = span(n)
    y = rgv[:, :, :, :, at].reshape(depth, 256)
    yh, yl = split(y)
    coef = accv[nl:, at] + (mm(qth[...], yh) + mm(qtl[...], yh) + mm(qth[...], yl))
    ch, cl = split(coef)
    r3 = jnp.concatenate([yh, yh, yl, ch, ch, cl], axis=0)
    out[...] = accv[0:nl, at] + mm(lt3[...], r3)
    qh, qlo = qrs[:, 0:ka], qrs[:, ka:]
    right_o[...] = rv[:, at] - (mm(qh, ch) + mm(qlo, ch) + mm(qh, cl))
    base = 3 * depth
    lh = lt3[at, base : base + ka]
    ll = lt3[at, base + ka : base + 2 * ka]
    qh, qlo = qls[:, 0:ka], qls[:, ka:]
    left_o[...] = lv[:, at] + (nt(qh, lh) + nt(qlo, lh) + nt(qh, ll))


def finish(acc, lg, rg, left, right, basis, rows, cols):
    ml, nl = left.shape
    mr, nr = right.shape
    ka = basis.shape[1]
    steps, _, lr, _ = lg.shape
    last = steps // GROUP - 1
    depth = GROUP * cols * lr
    basis3 = basis.reshape(cols, ml, ka)
    basis4 = basis.reshape(rows, mr, ka)
    tiles = nr // 256
    tile = lambda height: pl.BlockSpec((height, 256), lambda n: (0, n))
    once = lambda shape, index: pl.BlockSpec(shape, index, pipeline_mode=pl.Buffered(1))
    any_spec = pl.BlockSpec(memory_space=pl.ANY)
    dma = pltpu.SemaphoreType.DMA
    return pl.pallas_call(
        finish_kernel,
        grid=(tiles,),
        out_shape=(
            jax.ShapeDtypeStruct((nl, nr), F32),
            jax.ShapeDtypeStruct((ml, nl), F32),
            jax.ShapeDtypeStruct((mr, nr), F32),
        ),
        in_specs=[
            any_spec,
            any_spec,
            any_spec,
            once((cols, GROUP * lr, ka), lambda n: (0, last, 0)),
            any_spec,
            any_spec,
            once((1, ml, ka), lambda n: (lax.axis_index("col"), 0, 0)),
            once((1, mr, ka), lambda n: (lax.axis_index("row"), 0, 0)),
        ],
        out_specs=[tile(nl), tile(ml), tile(mr)],
        scratch_shapes=[
            pltpu.VMEM((nl, 3 * depth + 3 * ka), BF16),
            pltpu.VMEM((ka, depth), BF16),
            pltpu.VMEM((ka, depth), BF16),
            pltpu.VMEM((ml, 2 * ka), BF16),
            pltpu.VMEM((mr, 2 * ka), BF16),
            pltpu.VMEM((nl + ka, nr), F32),
            pltpu.VMEM((nl, ka), F32),
            pltpu.VMEM((GROUP, cols, lr, nl), F32),
            pltpu.VMEM((GROUP, rows, cols // rows, lr, nr), F32),
            pltpu.VMEM((ml, nl), F32),
            pltpu.VMEM((mr, nr), F32),
            dma((4, tiles)),
            dma((2, nl // 256)),
        ],
        compiler_params=pltpu.CompilerParams(
            dimension_semantics=("arbitrary",), vmem_limit_bytes=64000 * 1024
        ),
        name="finish",
    )(acc, lg, rg, basis3, left, right, basis3, basis4)


def fast(rows, cols, left, right, basis, block):
    acc, lg, rg = gather_product(left, right, basis, block, rows, cols)
    return finish(acc, lg, rg, left, right, basis, rows, cols)


def plain(left, right, basis, block):
    ml = left.shape[0]
    mr = right.shape[0]
    whole_left = lax.all_gather(left, "col", axis=0, tiled=True)
    whole_right = lax.all_gather(right, "row", axis=0, tiled=True)
    bl = lax.dynamic_slice_in_dim(basis, lax.axis_index("col") * ml, ml, 0)
    br = lax.dynamic_slice_in_dim(basis, lax.axis_index("row") * mr, mr, 0)
    lc = dot(basis, whole_left, ((0,), (0,)))
    rc = dot(basis, whole_right, ((0,), (0,)))
    updated = block + dot(whole_left, whole_right, ((0,), (0,))) - dot(lc, rc, ((0,), (0,)))
    left_reduced = left - dot(bl, lc, ((1,), (0,)))
    right_reduced = right - dot(br, rc, ((1,), (0,)))
    return updated, left_reduced, right_reduced


def solution(mesh):
    rows, cols = mesh.shape["row"], mesh.shape["col"]
    local = functools.partial(fast, rows, cols) if (rows, cols) == (4, 8) else plain
    in_specs = (P("col", "row"), P("row", "col"), P(), P("row", "col"))
    out_specs = (P("row", "col"), P("col", "row"), P("row", "col"))
    return jax.shard_map(
        local, mesh=mesh, in_specs=in_specs, out_specs=out_specs, check_vma=False
    )
```

```python
import functools

import jax
import jax.numpy as jnp
from jax import lax
from jax.experimental import pallas as pl
from jax.experimental.pallas import tpu as pltpu
from jax.sharding import PartitionSpec as P

COMM = True
COMPUTE = True
STEPS = 32
GROUP = 2
CUT1 = 0
CUT2 = 3
CUT3 = 5

MESH = pl.DeviceIdType.MESH
F32 = jnp.float32
BF16 = jnp.bfloat16


def split(x):
    hi = x.astype(BF16)
    lo = (x - hi.astype(F32)).astype(BF16)
    return hi, lo


def kernel(
    steps, left, right, basis, block, acc_o, lg, rg,
    acc, lbuf, rbuf, qv, lt3, r3, ltail, rtail,
    s_own, s_relay, s_fwd, s_right, r_left, r_fwd, r_right, ld_sem, misc, tail_sem, out_sem,
):
    r = lax.axis_index("row")
    c = lax.axis_index("col")
    z = c // 2
    k = c % 2
    sib = c + 1 - 2 * k
    rx = r + 1 - 2 * (r % 2)
    ry = (r + 2) % 4
    lr = lbuf.shape[3]
    nl = left.shape[1]
    nr = right.shape[2]
    ka = basis.shape[2]

    def remote(src, dst, ss, rs, row, col):
        return pltpu.make_async_remote_copy(
            src_ref=src, dst_ref=dst, send_sem=ss, recv_sem=rs,
            device_id={"row": row, "col": col}, device_id_type=MESH,
        )

    def mine(s):
        return left.at[pl.ds(pl.multiple_of(s * lr, lr), lr), :]

    def own_up(s):
        return remote(mine(s), lg.at[s, c], s_own.at[s, 0], r_left.at[s, z], r, c + 2)

    def own_dn(s):
        return remote(mine(s), lg.at[s, c], s_own.at[s, 1], r_left.at[s, z], r, c - 2)

    def own_far(s):
        far = 6 + k - 6 * (z // 3)
        return remote(mine(s), lg.at[s, c], s_own.at[s, 2], r_left.at[s, z], r, far)

    def relay_up(s):
        return remote(lg.at[s, c - 2], lg.at[s, c - 2], s_relay.at[s, 0], r_left.at[s, z - 1], r, c + 2)

    def relay_dn(s):
        return remote(lg.at[s, c + 2], lg.at[s, c + 2], s_relay.at[s, 1], r_left.at[s, z + 1], r, c - 2)

    def fwd_own(s):
        return remote(mine(s), lg.at[s, c], s_fwd.at[s, z], r_fwd.at[s, z], r, sib)

    def fwd(s, o):
        at = lg.at[s, 2 * o + k]
        return remote(at, at, s_fwd.at[s, o], r_fwd.at[s, o], r, sib)

    def arrived(s, o):
        at = lg.at[s, 2 * o + k]
        return remote(at, at, s_fwd.at[s, o], r_left.at[s, o], r, sib)

    def own_r(s, i, row):
        src = right.at[:, pl.ds(pl.multiple_of(s * lr, lr), lr), :]
        return remote(src, rg.at[s, r], s_right.at[s, i], r_right.at[s, i], row, c)

    def relay_r(s, i, owner, row):
        at = rg.at[s, owner, i]
        return remote(at, at, s_right.at[s, 2 + i], r_right.at[s, 2 + i], row, c)

    def start_own(s):
        own_r(s, 0, rx).start()
        own_r(s, 1, ry).start()

        @pl.when(z < 3)
        def _():
            own_up(s).start()

        @pl.when(z > 0)
        def _():
            own_dn(s).start()

        @pl.when(z % 3 == 0)
        def _():
            own_far(s).start()

        fwd_own(s).start()

    def stage1(s):
        own_r(s, 0, rx).wait_recv()
        relay_r(s, 0, rx, ry).start()
        own_r(s, 1, ry).wait_recv()
        relay_r(s, 1, ry, rx).start()

        @pl.when(z > 0)
        def _():
            arrived(s, z - 1).wait_recv()

            @pl.when(z < 3)
            def _():
                relay_up(s).start()

            fwd(s, z - 1).start()

        @pl.when(z < 3)
        def _():
            arrived(s, z + 1).wait_recv()

            @pl.when(z > 0)
            def _():
                relay_dn(s).start()

            fwd(s, z + 1).start()

    def stage2(s):
        far = (z + 2) % 4
        arrived(s, far).wait_recv()
        fwd(s, far).start()

        @pl.when(z % 3 == 0)
        def _():
            end = 3 - z
            arrived(s, end).wait_recv()
            fwd(s, end).start()

        relay_r(s, 0, rx, ry).wait_recv()
        relay_r(s, 1, ry, rx).wait_recv()

    def stage3(s):
        @pl.loop(0, 4)
        def _(o):
            at = lg.at[s, 2 * o + 1 - k]
            remote(at, at, s_fwd.at[s, o], r_fwd.at[s, o], r, sib).wait_recv()

    def sent(s):
        own_r(s, 0, rx).wait_send()
        own_r(s, 1, ry).wait_send()
        relay_r(s, 0, rx, ry).wait_send()
        relay_r(s, 1, ry, rx).wait_send()
        fwd_own(s).wait_send()

        @pl.loop(1, 4)
        def _(d):
            fwd(s, (z + d) % 4).wait_send()

        @pl.when(z < 3)
        def _():
            own_up(s).wait_send()

        @pl.when(z > 0)
        def _():
            own_dn(s).wait_send()

        @pl.when(z % 3 == 0)
        def _():
            own_far(s).wait_send()

        @pl.when((z > 0) & (z < 3))
        def _():
            relay_up(s).wait_send()
            relay_dn(s).wait_send()

    def load(s):
        slot = (s // GROUP) % 2
        i = s % GROUP
        pltpu.make_async_copy(mine(s), lbuf.at[slot, i, c], ld_sem.at[0, slot, i]).start()
        src = right.at[:, pl.ds(pl.multiple_of(s * lr, lr), lr), :]
        pltpu.make_async_copy(src, rbuf.at[slot, i, r], ld_sem.at[1, slot, i]).start()

        @pl.loop(1, 8)
        def _(d):
            o = (c + d) % 8
            pltpu.make_async_copy(lg.at[s, o], lbuf.at[slot, i, o], ld_sem.at[0, slot, i]).start()

        @pl.loop(1, 4)
        def _(d):
            o = (r + d) % 4
            pltpu.make_async_copy(rg.at[s, o], rbuf.at[slot, i, o], ld_sem.at[1, slot, i]).start()

    def loaded(s):
        slot = (s // GROUP) % 2
        i = s % GROUP
        pltpu.make_async_copy(lg.at[s], lbuf.at[slot, i], ld_sem.at[0, slot, i]).wait()
        pltpu.make_async_copy(rg.at[s], rbuf.at[slot, i], ld_sem.at[1, slot, i]).wait()

    depth = GROUP * 8 * lr

    def put_left(x, at):
        hi, lo = split(x.T)
        lt3[pl.ds(at, 256), 0:depth] = hi
        lt3[pl.ds(at, 256), depth : 2 * depth] = lo
        lt3[pl.ds(at, 256), 2 * depth : 3 * depth] = hi

    def put_right(x, at):
        hi, lo = split(x)
        r3[0:depth, pl.ds(at, 256)] = hi
        r3[depth : 2 * depth, pl.ds(at, 256)] = hi
        r3[2 * depth : 3 * depth, pl.ds(at, 256)] = lo

    def prepare(j):
        slot = j % 2

        @pl.loop(0, nl // 256)
        def _(b):
            at = pl.multiple_of(b * 256, 256)
            put_left(lbuf[slot, :, :, :, pl.ds(at, 256)].reshape(depth, 256), at)

        @pl.loop(0, nr // 256)
        def _(b):
            at = pl.multiple_of(b * 256, 256)
            put_right(rbuf[slot, :, :, :, :, pl.ds(at, 256)].reshape(depth, 256), at)

        q = qv[:, pl.ds(pl.multiple_of(j * GROUP * lr, GROUP * lr), GROUP * lr), :]
        q = jnp.concatenate(
            [q[:, i * lr : (i + 1) * lr].reshape(8 * lr, ka) for i in range(GROUP)], axis=0
        )
        put_left(q, nl)
        put_right(q, nr)

    tiles_n = (nr + ka) // 256

    def columns(n):
        return pl.ds(pl.multiple_of((n + tiles_n - 1) % tiles_n * 256, 256), 256)

    def out_tile(n):
        cols = columns(n)
        return pltpu.make_async_copy(acc.at[:, cols], acc_o.at[:, cols], out_sem.at[n])

    if True:
        barrier = pltpu.get_barrier_semaphore()
        za = (z + 1) % 4
        zb = (z + 3) % 4
        for row, col in ((rx, c), (ry, c), (r, sib), (r, 2 * za + k), (r, 2 * zb + k)):
            pl.semaphore_signal(barrier, inc=1, device_id={"row": row, "col": col}, device_id_type=MESH)
        pl.semaphore_wait(barrier, 5)
    if COMM:
        for s in range(GROUP):
            start_own(s)

    fill = pltpu.make_async_copy(block, acc.at[0:nl, 0:nr], misc.at[0])
    fill.start()
    qfill = pltpu.make_async_copy(basis, qv, misc.at[1])
    qfill.start()
    acc[nl:, :] = jnp.zeros((ka, nr + ka), F32)
    acc[0:nl, nr:] = jnp.zeros((nl, ka), F32)

    first = steps - GROUP
    tail_in = []
    tail_out = []
    for i in range(GROUP):
        at = pl.ds((first + i) * lr, lr)
        tail_in += [
            pltpu.make_async_copy(left.at[at, :], ltail.at[i], tail_sem.at[0, i]),
            pltpu.make_async_copy(right.at[:, at, :], rtail.at[i], tail_sem.at[1, i]),
        ]
        tail_out += [
            pltpu.make_async_copy(ltail.at[i], lg.at[first + i, c], tail_sem.at[2, i]),
            pltpu.make_async_copy(rtail.at[i], rg.at[first + i, r], tail_sem.at[3, i]),
        ]
    for copy in tail_in:
        copy.start()

    end = steps - GROUP

    @pl.loop(0, steps // GROUP)
    def _(h):
        t = h * GROUP

        if COMM:
            stage1(t)

            @pl.when(t > 0)
            def _():
                stage3(t - 2)

            @pl.when(t > GROUP)
            def _():
                sent(t - 4)
                sent(t - 3)
        if COMPUTE:
            @pl.when(t > 0)
            def _():
                load(t - 2)
        if COMM:
            @pl.when(t > 0)
            def _():
                stage2(t - 1)
                stage3(t - 1)
        if COMPUTE:
            @pl.when(t > 0)
            def _():
                load(t - 1)
        if COMM:
            @pl.when(t < end)
            def _():
                start_own(t + 2)

        if COMPUTE:
            @pl.when(t == GROUP)
            def _():
                fill.wait()
                qfill.wait()
                for copy in tail_in:
                    copy.wait()
                for copy in tail_out:
                    copy.start()

            @pl.when(t > 0)
            def _():
                loaded(t - 2)
                loaded(t - 1)
                prepare(h - 1)

        @pl.loop(0, tiles_n)
        def _(n):
            if COMPUTE:
                @pl.when(t > 0)
                def _():
                    cols = columns(n)
                    acc[:, cols] += jnp.dot(lt3[...], r3[:, cols], preferred_element_type=F32)

                @pl.when(t == end)
                def _():
                    out_tile(n).start()

            if COMM:
                @pl.when(n == CUT1)
                def _():
                    stage1(t + 1)

                @pl.when(n == CUT2)
                def _():
                    stage2(t)

                    @pl.when(t < end)
                    def _():
                        start_own(t + 3)

                @pl.when((n == CUT3) & (t == end))
                def _():
                    stage2(t + 1)

    if COMM:
        for s in range(end, steps):
            stage3(s)

    if COMM:
        for s in range(end - GROUP, steps):
            sent(s)

    if not COMPUTE:
        for copy in tail_in + [fill, qfill]:
            copy.wait()
    if COMPUTE:
        for copy in tail_out:
            copy.wait()

        @pl.loop(0, tiles_n)
        def _(n):
            out_tile(n).wait()


def gather_product(left, right, basis, block, rows, cols):
    steps = STEPS
    ml, nl = left.shape
    mr, nr = right.shape
    ka = basis.shape[1]
    lr = ml // steps
    right3 = right.reshape(cols // rows, ml, nr)
    basis3 = basis.reshape(cols, ml, ka)
    any_spec = pl.BlockSpec(memory_space=pl.ANY)
    dma = pltpu.SemaphoreType.DMA
    return pl.pallas_call(
        functools.partial(kernel, steps),
        out_shape=(
            jax.ShapeDtypeStruct((nl + ka, nr + ka), F32),
            jax.ShapeDtypeStruct((steps, cols, lr, nl), F32),
            jax.ShapeDtypeStruct((steps, rows, cols // rows, lr, nr), F32),
        ),
        in_specs=[any_spec] * 4,
        out_specs=[any_spec] * 3,
        scratch_shapes=[
            pltpu.VMEM((nl + ka, nr + ka), F32),
            pltpu.VMEM((2, GROUP, cols, lr, nl), F32),
            pltpu.VMEM((2, GROUP, rows, cols // rows, lr, nr), F32),
            pltpu.VMEM((cols, ml, ka), F32),
            pltpu.VMEM((nl + ka, 3 * GROUP * cols * lr), BF16),
            pltpu.VMEM((3 * GROUP * cols * lr, nr + ka), BF16),
            pltpu.VMEM((GROUP, lr, nl), F32),
            pltpu.VMEM((GROUP, cols // rows, lr, nr), F32),
            dma((steps, 3)),
            dma((steps, 2)),
            dma((steps, 4)),
            dma((steps, 4)),
            dma((steps, 4)),
            dma((steps, 4)),
            dma((steps, 4)),
            dma((2, 2, GROUP)),
            dma((2,)),
            dma((4, GROUP)),
            dma(((nr + ka) // 256,)),
        ],
        compiler_params=pltpu.CompilerParams(
            collective_id=0, has_side_effects=True, vmem_limit_bytes=64000 * 1024
        ),
        name="gather_product",
    )(left, right3, basis3, block)


def dot(a, b, dims):
    return lax.dot_general(
        a, b, (dims, ((), ())), precision=lax.Precision.HIGH, preferred_element_type=F32
    )


def finish_kernel(
    acc, lg, rg, qt, left, right, ql, qr, out, left_o, right_o,
    lt3, qth, qtl, qls, qrs, accv, lctv, lgv, rgv, lv, rv, sem, sem_l,
):
    n = pl.program_id(0)
    group, parts, lr = lgv.shape[0], lgv.shape[1], lgv.shape[2]
    depth = group * parts * lr
    ka = qth.shape[0]
    nl = lgv.shape[3]
    nr = rv.shape[1]
    last = lg.shape[0] // group - 1
    mm = functools.partial(jnp.dot, preferred_element_type=F32)

    def nt(a, b):
        return lax.dot_general(a, b, (((1,), (1,)), ((), ())), preferred_element_type=F32)

    def span(i):
        return pl.ds(pl.multiple_of(i * 256, 256), 256)

    tail = pl.ds(last * group, group)

    def left_in(b):
        at = span(b)
        return (
            pltpu.make_async_copy(acc.at[at, nr:], lctv.at[at, :], sem_l.at[0, b]),
            pltpu.make_async_copy(lg.at[tail, :, :, at], lgv.at[:, :, :, at], sem_l.at[1, b]),
        )

    def tile_in(i):
        at = span(i)
        return (
            pltpu.make_async_copy(rg.at[tail, :, :, :, at], rgv.at[:, :, :, :, at], sem.at[0, i]),
            pltpu.make_async_copy(acc.at[:, at], accv.at[:, at], sem.at[1, i]),
            pltpu.make_async_copy(right.at[:, at], rv.at[:, at], sem.at[2, i]),
            pltpu.make_async_copy(left.at[:, at], lv.at[:, at], sem.at[3, i]),
        )

    @pl.when(n == 0)
    def _():
        @pl.loop(0, nl // 256)
        def _(b):
            for copy in left_in(b):
                copy.start()

        @pl.loop(0, nr // 256)
        def _(i):
            for copy in tile_in(i):
                copy.start()

        q = jnp.concatenate(
            [qt[:, i * lr : (i + 1) * lr].reshape(parts * lr, ka) for i in range(group)], axis=0
        )
        qh, qlo = split(q)
        hi, lo = split(q.T)
        qth[...] = hi
        qtl[...] = lo
        hi, lo = split(ql[0])
        qls[:, 0:ka] = hi
        qls[:, ka:] = lo
        hi, lo = split(qr[0])
        qrs[:, 0:ka] = hi
        qrs[:, ka:] = lo

        @pl.loop(0, nl // 256)
        def _(b):
            for copy in left_in(b):
                copy.wait()
            at = span(b)
            hi, lo = split(lgv[:, :, :, at].reshape(depth, 256).T)
            lt3[at, 0:depth] = hi
            lt3[at, depth : 2 * depth] = lo
            lt3[at, 2 * depth : 3 * depth] = hi
            coef = lctv[at, :] + (mm(hi, qh) + mm(lo, qh) + mm(hi, qlo))
            hi, lo = split(-coef)
            base = 3 * depth
            lt3[at, base : base + ka] = hi
            lt3[at, base + ka : base + 2 * ka] = lo
            lt3[at, base + 2 * ka :] = hi

    for copy in tile_in(n):
        copy.wait()
    at = span(n)
    y = rgv[:, :, :, :, at].reshape(depth, 256)
    yh, yl = split(y)
    coef = accv[nl:, at] + (mm(qth[...], yh) + mm(qtl[...], yh) + mm(qth[...], yl))
    ch, cl = split(coef)
    r3 = jnp.concatenate([yh, yh, yl, ch, ch, cl], axis=0)
    out[...] = accv[0:nl, at] + mm(lt3[...], r3)
    qh, qlo = qrs[:, 0:ka], qrs[:, ka:]
    right_o[...] = rv[:, at] - (mm(qh, ch) + mm(qlo, ch) + mm(qh, cl))
    base = 3 * depth
    lh = lt3[at, base : base + ka]
    ll = lt3[at, base + ka : base + 2 * ka]
    qh, qlo = qls[:, 0:ka], qls[:, ka:]
    left_o[...] = lv[:, at] + (nt(qh, lh) + nt(qlo, lh) + nt(qh, ll))


def finish(acc, lg, rg, left, right, basis, rows, cols):
    ml, nl = left.shape
    mr, nr = right.shape
    ka = basis.shape[1]
    steps, _, lr, _ = lg.shape
    last = steps // GROUP - 1
    depth = GROUP * cols * lr
    basis3 = basis.reshape(cols, ml, ka)
    basis4 = basis.reshape(rows, mr, ka)
    tiles = nr // 256
    tile = lambda height: pl.BlockSpec((height, 256), lambda n: (0, n))
    once = lambda shape, index: pl.BlockSpec(shape, index, pipeline_mode=pl.Buffered(1))
    any_spec = pl.BlockSpec(memory_space=pl.ANY)
    dma = pltpu.SemaphoreType.DMA
    return pl.pallas_call(
        finish_kernel,
        grid=(tiles,),
        out_shape=(
            jax.ShapeDtypeStruct((nl, nr), F32),
            jax.ShapeDtypeStruct((ml, nl), F32),
            jax.ShapeDtypeStruct((mr, nr), F32),
        ),
        in_specs=[
            any_spec,
            any_spec,
            any_spec,
            once((cols, GROUP * lr, ka), lambda n: (0, last, 0)),
            any_spec,
            any_spec,
            once((1, ml, ka), lambda n: (lax.axis_index("col"), 0, 0)),
            once((1, mr, ka), lambda n: (lax.axis_index("row"), 0, 0)),
        ],
        out_specs=[tile(nl), tile(ml), tile(mr)],
        scratch_shapes=[
            pltpu.VMEM((nl, 3 * depth + 3 * ka), BF16),
            pltpu.VMEM((ka, depth), BF16),
            pltpu.VMEM((ka, depth), BF16),
            pltpu.VMEM((ml, 2 * ka), BF16),
            pltpu.VMEM((mr, 2 * ka), BF16),
            pltpu.VMEM((nl + ka, nr), F32),
            pltpu.VMEM((nl, ka), F32),
            pltpu.VMEM((GROUP, cols, lr, nl), F32),
            pltpu.VMEM((GROUP, rows, cols // rows, lr, nr), F32),
            pltpu.VMEM((ml, nl), F32),
            pltpu.VMEM((mr, nr), F32),
            dma((4, tiles)),
            dma((2, nl // 256)),
        ],
        compiler_params=pltpu.CompilerParams(
            dimension_semantics=("arbitrary",), vmem_limit_bytes=64000 * 1024
        ),
        name="finish",
    )(acc, lg, rg, basis3, left, right, basis3, basis4)


def fast(rows, cols, left, right, basis, block):
    acc, lg, rg = gather_product(left, right, basis, block, rows, cols)
    return finish(acc, lg, rg, left, right, basis, rows, cols)


def plain(left, right, basis, block):
    ml = left.shape[0]
    mr = right.shape[0]
    whole_left = lax.all_gather(left, "col", axis=0, tiled=True)
    whole_right = lax.all_gather(right, "row", axis=0, tiled=True)
    bl = lax.dynamic_slice_in_dim(basis, lax.axis_index("col") * ml, ml, 0)
    br = lax.dynamic_slice_in_dim(basis, lax.axis_index("row") * mr, mr, 0)
    lc = dot(basis, whole_left, ((0,), (0,)))
    rc = dot(basis, whole_right, ((0,), (0,)))
    updated = block + dot(whole_left, whole_right, ((0,), (0,))) - dot(lc, rc, ((0,), (0,)))
    left_reduced = left - dot(bl, lc, ((1,), (0,)))
    right_reduced = right - dot(br, rc, ((1,), (0,)))
    return updated, left_reduced, right_reduced


def solution(mesh):
    rows, cols = mesh.shape["row"], mesh.shape["col"]
    local = functools.partial(fast, rows, cols) if (rows, cols) == (4, 8) else plain
    in_specs = (P("col", "row"), P("row", "col"), P(), P("row", "col"))
    out_specs = (P("row", "col"), P("col", "row"), P("row", "col"))
    return jax.shard_map(
        local, mesh=mesh, in_specs=in_specs, out_specs=out_specs, check_vma=False
    )
```

```python
import functools

import jax
import jax.numpy as jnp
from jax import lax
from jax.experimental import pallas as pl
from jax.experimental.pallas import tpu as pltpu
from jax.sharding import PartitionSpec as P

COMM = True
COMPUTE = True
STEPS = 32
GROUP = 2
CUT1 = 0
CUT2 = 3
CUT3 = 5

MESH = pl.DeviceIdType.MESH
F32 = jnp.float32
BF16 = jnp.bfloat16


def split(x):
    hi = x.astype(BF16)
    lo = (x - hi.astype(F32)).astype(BF16)
    return hi, lo


def kernel(
    steps, left, right, basis, block, acc_o, lg, rg,
    acc, lbuf, rbuf, qv, lt3, r3, ltail, rtail,
    s_own, s_relay, s_fwd, s_right, r_left, r_fwd, r_right, ld_sem, misc, tail_sem, out_sem,
):
    r = lax.axis_index("row")
    c = lax.axis_index("col")
    z = c // 2
    k = c % 2
    sib = c + 1 - 2 * k
    rx = r + 1 - 2 * (r % 2)
    ry = (r + 2) % 4
    lr = lbuf.shape[3]
    nl = left.shape[1]
    nr = right.shape[2]
    ka = basis.shape[2]

    def remote(src, dst, ss, rs, row, col):
        return pltpu.make_async_remote_copy(
            src_ref=src, dst_ref=dst, send_sem=ss, recv_sem=rs,
            device_id={"row": row, "col": col}, device_id_type=MESH,
        )

    def mine(s):
        return left.at[pl.ds(pl.multiple_of(s * lr, lr), lr), :]

    def own_up(s):
        return remote(mine(s), lg.at[s, c], s_own.at[s, 0], r_left.at[s, z], r, c + 2)

    def own_dn(s):
        return remote(mine(s), lg.at[s, c], s_own.at[s, 1], r_left.at[s, z], r, c - 2)

    def own_far(s):
        far = 6 + k - 6 * (z // 3)
        return remote(mine(s), lg.at[s, c], s_own.at[s, 2], r_left.at[s, z], r, far)

    def relay_up(s):
        return remote(lg.at[s, c - 2], lg.at[s, c - 2], s_relay.at[s, 0], r_left.at[s, z - 1], r, c + 2)

    def relay_dn(s):
        return remote(lg.at[s, c + 2], lg.at[s, c + 2], s_relay.at[s, 1], r_left.at[s, z + 1], r, c - 2)

    def fwd_own(s):
        return remote(mine(s), lg.at[s, c], s_fwd.at[s, z], r_fwd.at[s, z], r, sib)

    def fwd(s, o):
        at = lg.at[s, 2 * o + k]
        return remote(at, at, s_fwd.at[s, o], r_fwd.at[s, o], r, sib)

    def arrived(s, o):
        at = lg.at[s, 2 * o + k]
        return remote(at, at, s_fwd.at[s, o], r_left.at[s, o], r, sib)

    def own_r(s, i, row):
        src = right.at[:, pl.ds(pl.multiple_of(s * lr, lr), lr), :]
        return remote(src, rg.at[s, r], s_right.at[s, i], r_right.at[s, i], row, c)

    def relay_r(s, i, owner, row):
        at = rg.at[s, owner, i]
        return remote(at, at, s_right.at[s, 2 + i], r_right.at[s, 2 + i], row, c)

    def start_own(s):
        own_r(s, 0, rx).start()
        own_r(s, 1, ry).start()

        @pl.when(z < 3)
        def _():
            own_up(s).start()

        @pl.when(z > 0)
        def _():
            own_dn(s).start()

        @pl.when(z % 3 == 0)
        def _():
            own_far(s).start()

        fwd_own(s).start()

    def stage1(s):
        own_r(s, 0, rx).wait_recv()
        relay_r(s, 0, rx, ry).start()
        own_r(s, 1, ry).wait_recv()
        relay_r(s, 1, ry, rx).start()

        @pl.when(z > 0)
        def _():
            arrived(s, z - 1).wait_recv()

            @pl.when(z < 3)
            def _():
                relay_up(s).start()

            fwd(s, z - 1).start()

        @pl.when(z < 3)
        def _():
            arrived(s, z + 1).wait_recv()

            @pl.when(z > 0)
            def _():
                relay_dn(s).start()

            fwd(s, z + 1).start()

    def stage2(s):
        far = (z + 2) % 4
        arrived(s, far).wait_recv()
        fwd(s, far).start()

        @pl.when(z % 3 == 0)
        def _():
            end = 3 - z
            arrived(s, end).wait_recv()
            fwd(s, end).start()

        relay_r(s, 0, rx, ry).wait_recv()
        relay_r(s, 1, ry, rx).wait_recv()

    def stage3(s):
        @pl.loop(0, 4)
        def _(o):
            at = lg.at[s, 2 * o + 1 - k]
            remote(at, at, s_fwd.at[s, o], r_fwd.at[s, o], r, sib).wait_recv()

    def sent(s):
        own_r(s, 0, rx).wait_send()
        own_r(s, 1, ry).wait_send()
        relay_r(s, 0, rx, ry).wait_send()
        relay_r(s, 1, ry, rx).wait_send()
        fwd_own(s).wait_send()

        @pl.loop(1, 4)
        def _(d):
            fwd(s, (z + d) % 4).wait_send()

        @pl.when(z < 3)
        def _():
            own_up(s).wait_send()

        @pl.when(z > 0)
        def _():
            own_dn(s).wait_send()

        @pl.when(z % 3 == 0)
        def _():
            own_far(s).wait_send()

        @pl.when((z > 0) & (z < 3))
        def _():
            relay_up(s).wait_send()
            relay_dn(s).wait_send()

    def load(s):
        slot = (s // GROUP) % 2
        i = s % GROUP
        pltpu.make_async_copy(mine(s), lbuf.at[slot, i, c], ld_sem.at[0, slot, i]).start()
        src = right.at[:, pl.ds(pl.multiple_of(s * lr, lr), lr), :]
        pltpu.make_async_copy(src, rbuf.at[slot, i, r], ld_sem.at[1, slot, i]).start()

        @pl.loop(1, 8)
        def _(d):
            o = (c + d) % 8
            pltpu.make_async_copy(lg.at[s, o], lbuf.at[slot, i, o], ld_sem.at[0, slot, i]).start()

        @pl.loop(1, 4)
        def _(d):
            o = (r + d) % 4
            pltpu.make_async_copy(rg.at[s, o], rbuf.at[slot, i, o], ld_sem.at[1, slot, i]).start()

    def loaded(s):
        slot = (s // GROUP) % 2
        i = s % GROUP
        pltpu.make_async_copy(lg.at[s], lbuf.at[slot, i], ld_sem.at[0, slot, i]).wait()
        pltpu.make_async_copy(rg.at[s], rbuf.at[slot, i], ld_sem.at[1, slot, i]).wait()

    depth = GROUP * 8 * lr

    def put_left(x, at):
        hi, lo = split(x.T)
        lt3[pl.ds(at, 256), 0:depth] = hi
        lt3[pl.ds(at, 256), depth : 2 * depth] = lo
        lt3[pl.ds(at, 256), 2 * depth : 3 * depth] = hi

    def put_right(x, at):
        hi, lo = split(x)
        r3[0:depth, pl.ds(at, 256)] = hi
        r3[depth : 2 * depth, pl.ds(at, 256)] = hi
        r3[2 * depth : 3 * depth, pl.ds(at, 256)] = lo

    def prepare(j):
        slot = j % 2

        @pl.loop(0, nl // 256)
        def _(b):
            at = pl.multiple_of(b * 256, 256)
            put_left(lbuf[slot, :, :, :, pl.ds(at, 256)].reshape(depth, 256), at)

        @pl.loop(0, nr // 256)
        def _(b):
            at = pl.multiple_of(b * 256, 256)
            put_right(rbuf[slot, :, :, :, :, pl.ds(at, 256)].reshape(depth, 256), at)

        q = qv[:, pl.ds(pl.multiple_of(j * GROUP * lr, GROUP * lr), GROUP * lr), :]
        q = jnp.concatenate(
            [q[:, i * lr : (i + 1) * lr].reshape(8 * lr, ka) for i in range(GROUP)], axis=0
        )
        put_left(q, nl)
        put_right(q, nr)

    tiles_n = (nr + ka) // 256

    def columns(n):
        return pl.ds(pl.multiple_of((n + tiles_n - 1) % tiles_n * 256, 256), 256)

    def out_tile(n):
        cols = columns(n)
        return pltpu.make_async_copy(acc.at[:, cols], acc_o.at[:, cols], out_sem.at[n])

    if True:
        barrier = pltpu.get_barrier_semaphore()
        za = (z + 1) % 4
        zb = (z + 3) % 4
        for row, col in ((rx, c), (ry, c), (r, sib), (r, 2 * za + k), (r, 2 * zb + k)):
            pl.semaphore_signal(barrier, inc=1, device_id={"row": row, "col": col}, device_id_type=MESH)
        pl.semaphore_wait(barrier, 5)
    if COMM:
        for s in range(GROUP):
            start_own(s)

    fill = pltpu.make_async_copy(block, acc.at[0:nl, 0:nr], misc.at[0])
    fill.start()
    qfill = pltpu.make_async_copy(basis, qv, misc.at[1])
    qfill.start()
    acc[nl:, :] = jnp.zeros((ka, nr + ka), F32)
    acc[0:nl, nr:] = jnp.zeros((nl, ka), F32)

    first = steps - GROUP
    tail_in = []
    tail_out = []
    for i in range(GROUP):
        at = pl.ds((first + i) * lr, lr)
        tail_in += [
            pltpu.make_async_copy(left.at[at, :], ltail.at[i], tail_sem.at[0, i]),
            pltpu.make_async_copy(right.at[:, at, :], rtail.at[i], tail_sem.at[1, i]),
        ]
        tail_out += [
            pltpu.make_async_copy(ltail.at[i], lg.at[first + i, c], tail_sem.at[2, i]),
            pltpu.make_async_copy(rtail.at[i], rg.at[first + i, r], tail_sem.at[3, i]),
        ]
    for copy in tail_in:
        copy.start()

    end = steps - GROUP

    @pl.loop(0, steps // GROUP)
    def _(h):
        t = h * GROUP

        if COMM:
            stage1(t)

            @pl.when(t > 0)
            def _():
                stage3(t - 2)

            @pl.when(t > GROUP)
            def _():
                sent(t - 4)
                sent(t - 3)
        if COMPUTE:
            @pl.when(t > 0)
            def _():
                load(t - 2)
        if COMM:
            @pl.when(t > 0)
            def _():
                stage2(t - 1)
                stage3(t - 1)
        if COMPUTE:
            @pl.when(t > 0)
            def _():
                load(t - 1)
        if COMM:
            @pl.when(t < end)
            def _():
                start_own(t + 2)

        if COMPUTE:
            @pl.when(t == GROUP)
            def _():
                fill.wait()
                qfill.wait()
                for copy in tail_in:
                    copy.wait()
                for copy in tail_out:
                    copy.start()

            @pl.when(t > 0)
            def _():
                loaded(t - 2)
                loaded(t - 1)
                prepare(h - 1)

        @pl.loop(0, tiles_n)
        def _(n):
            if COMPUTE:
                @pl.when(t > 0)
                def _():
                    cols = columns(n)
                    acc[:, cols] += jnp.dot(lt3[...], r3[:, cols], preferred_element_type=F32)

                @pl.when(t == end)
                def _():
                    out_tile(n).start()

            if COMM:
                @pl.when(n == CUT1)
                def _():
                    stage1(t + 1)

                @pl.when(n == CUT2)
                def _():
                    stage2(t)

                    @pl.when(t < end)
                    def _():
                        start_own(t + 3)

                @pl.when((n == CUT3) & (t == end))
                def _():
                    stage2(t + 1)

    if COMM:
        for s in range(end, steps):
            stage3(s)

    if COMM:
        for s in range(end - GROUP, steps):
            sent(s)

    if not COMPUTE:
        for copy in tail_in + [fill, qfill]:
            copy.wait()
    if COMPUTE:
        for copy in tail_out:
            copy.wait()

        @pl.loop(0, tiles_n)
        def _(n):
            out_tile(n).wait()


def gather_product(left, right, basis, block, rows, cols):
    steps = STEPS
    ml, nl = left.shape
    mr, nr = right.shape
    ka = basis.shape[1]
    lr = ml // steps
    right3 = right.reshape(cols // rows, ml, nr)
    basis3 = basis.reshape(cols, ml, ka)
    any_spec = pl.BlockSpec(memory_space=pl.ANY)
    dma = pltpu.SemaphoreType.DMA
    return pl.pallas_call(
        functools.partial(kernel, steps),
        out_shape=(
            jax.ShapeDtypeStruct((nl + ka, nr + ka), F32),
            jax.ShapeDtypeStruct((steps, cols, lr, nl), F32),
            jax.ShapeDtypeStruct((steps, rows, cols // rows, lr, nr), F32),
        ),
        in_specs=[any_spec] * 4,
        out_specs=[any_spec] * 3,
        scratch_shapes=[
            pltpu.VMEM((nl + ka, nr + ka), F32),
            pltpu.VMEM((2, GROUP, cols, lr, nl), F32),
            pltpu.VMEM((2, GROUP, rows, cols // rows, lr, nr), F32),
            pltpu.VMEM((cols, ml, ka), F32),
            pltpu.VMEM((nl + ka, 3 * GROUP * cols * lr), BF16),
            pltpu.VMEM((3 * GROUP * cols * lr, nr + ka), BF16),
            pltpu.VMEM((GROUP, lr, nl), F32),
            pltpu.VMEM((GROUP, cols // rows, lr, nr), F32),
            dma((steps, 3)),
            dma((steps, 2)),
            dma((steps, 4)),
            dma((steps, 4)),
            dma((steps, 4)),
            dma((steps, 4)),
            dma((steps, 4)),
            dma((2, 2, GROUP)),
            dma((2,)),
            dma((4, GROUP)),
            dma(((nr + ka) // 256,)),
        ],
        compiler_params=pltpu.CompilerParams(
            collective_id=0, has_side_effects=True, vmem_limit_bytes=64000 * 1024
        ),
        name="gather_product",
    )(left, right3, basis3, block)


def dot(a, b, dims):
    return lax.dot_general(
        a, b, (dims, ((), ())), precision=lax.Precision.HIGH, preferred_element_type=F32
    )


def finish_kernel(
    acc, lg, rg, qt, left, right, ql, qr, out, left_o, right_o,
    lt3, qth, qtl, qls, qrs, accv, lctv, lgv, rgv, lv, rv, sem, sem_l,
):
    n = pl.program_id(0)
    group, parts, lr = lgv.shape[0], lgv.shape[1], lgv.shape[2]
    depth = group * parts * lr
    ka = qth.shape[0]
    nl = lgv.shape[3]
    nr = rv.shape[1]
    last = lg.shape[0] // group - 1
    mm = functools.partial(jnp.dot, preferred_element_type=F32)

    def nt(a, b):
        return lax.dot_general(a, b, (((1,), (1,)), ((), ())), preferred_element_type=F32)

    def span(i):
        return pl.ds(pl.multiple_of(i * 256, 256), 256)

    tail = pl.ds(last * group, group)

    def left_in(b):
        at = span(b)
        return (
            pltpu.make_async_copy(acc.at[at, nr:], lctv.at[at, :], sem_l.at[0, b]),
            pltpu.make_async_copy(lg.at[tail, :, :, at], lgv.at[:, :, :, at], sem_l.at[1, b]),
        )

    def tile_in(i):
        at = span(i)
        return (
            pltpu.make_async_copy(rg.at[tail, :, :, :, at], rgv.at[:, :, :, :, at], sem.at[0, i]),
            pltpu.make_async_copy(acc.at[:, at], accv.at[:, at], sem.at[1, i]),
            pltpu.make_async_copy(right.at[:, at], rv.at[:, at], sem.at[2, i]),
            pltpu.make_async_copy(left.at[:, at], lv.at[:, at], sem.at[3, i]),
        )

    @pl.when(n == 0)
    def _():
        @pl.loop(0, nl // 256)
        def _(b):
            for copy in left_in(b):
                copy.start()

        @pl.loop(0, nr // 256)
        def _(i):
            for copy in tile_in(i):
                copy.start()

        q = jnp.concatenate(
            [qt[:, i * lr : (i + 1) * lr].reshape(parts * lr, ka) for i in range(group)], axis=0
        )
        qh, qlo = split(q)
        hi, lo = split(q.T)
        qth[...] = hi
        qtl[...] = lo
        hi, lo = split(ql[0])
        qls[:, 0:ka] = hi
        qls[:, ka:] = lo
        hi, lo = split(qr[0])
        qrs[:, 0:ka] = hi
        qrs[:, ka:] = lo

        @pl.loop(0, nl // 256)
        def _(b):
            for copy in left_in(b):
                copy.wait()
            at = span(b)
            hi, lo = split(lgv[:, :, :, at].reshape(depth, 256).T)
            lt3[at, 0:depth] = hi
            lt3[at, depth : 2 * depth] = lo
            lt3[at, 2 * depth : 3 * depth] = hi

        q3 = jnp.concatenate([qh, qh, qlo], axis=0)
        base = 3 * depth
        coef = lctv[...] + mm(lt3[:, 0:base], q3)
        hi, lo = split(-coef)
        lt3[:, base : base + ka] = hi
        lt3[:, base + ka : base + 2 * ka] = lo
        lt3[:, base + 2 * ka :] = hi

    for copy in tile_in(n):
        copy.wait()
    at = span(n)
    y = rgv[:, :, :, :, at].reshape(depth, 256)
    yh, yl = split(y)
    coef = accv[nl:, at] + (mm(qth[...], yh) + mm(qtl[...], yh) + mm(qth[...], yl))
    ch, cl = split(coef)
    r3 = jnp.concatenate([yh, yh, yl, ch, ch, cl], axis=0)
    out[...] = accv[0:nl, at] + mm(lt3[...], r3)
    qh, qlo = qrs[:, 0:ka], qrs[:, ka:]
    right_o[...] = rv[:, at] - (mm(qh, ch) + mm(qlo, ch) + mm(qh, cl))
    base = 3 * depth
    lh = lt3[at, base : base + ka]
    ll = lt3[at, base + ka : base + 2 * ka]
    qh, qlo = qls[:, 0:ka], qls[:, ka:]
    left_o[...] = lv[:, at] + (nt(qh, lh) + nt(qlo, lh) + nt(qh, ll))


def finish(acc, lg, rg, left, right, basis, rows, cols):
    ml, nl = left.shape
    mr, nr = right.shape
    ka = basis.shape[1]
    steps, _, lr, _ = lg.shape
    last = steps // GROUP - 1
    depth = GROUP * cols * lr
    basis3 = basis.reshape(cols, ml, ka)
    basis4 = basis.reshape(rows, mr, ka)
    tiles = nr // 256
    tile = lambda height: pl.BlockSpec((height, 256), lambda n: (0, n))
    once = lambda shape, index: pl.BlockSpec(shape, index, pipeline_mode=pl.Buffered(1))
    any_spec = pl.BlockSpec(memory_space=pl.ANY)
    dma = pltpu.SemaphoreType.DMA
    return pl.pallas_call(
        finish_kernel,
        grid=(tiles,),
        out_shape=(
            jax.ShapeDtypeStruct((nl, nr), F32),
            jax.ShapeDtypeStruct((ml, nl), F32),
            jax.ShapeDtypeStruct((mr, nr), F32),
        ),
        in_specs=[
            any_spec,
            any_spec,
            any_spec,
            once((cols, GROUP * lr, ka), lambda n: (0, last, 0)),
            any_spec,
            any_spec,
            once((1, ml, ka), lambda n: (lax.axis_index("col"), 0, 0)),
            once((1, mr, ka), lambda n: (lax.axis_index("row"), 0, 0)),
        ],
        out_specs=[tile(nl), tile(ml), tile(mr)],
        scratch_shapes=[
            pltpu.VMEM((nl, 3 * depth + 3 * ka), BF16),
            pltpu.VMEM((ka, depth), BF16),
            pltpu.VMEM((ka, depth), BF16),
            pltpu.VMEM((ml, 2 * ka), BF16),
            pltpu.VMEM((mr, 2 * ka), BF16),
            pltpu.VMEM((nl + ka, nr), F32),
            pltpu.VMEM((nl, ka), F32),
            pltpu.VMEM((GROUP, cols, lr, nl), F32),
            pltpu.VMEM((GROUP, rows, cols // rows, lr, nr), F32),
            pltpu.VMEM((ml, nl), F32),
            pltpu.VMEM((mr, nr), F32),
            dma((4, tiles)),
            dma((2, nl // 256)),
        ],
        compiler_params=pltpu.CompilerParams(
            dimension_semantics=("arbitrary",), vmem_limit_bytes=64000 * 1024
        ),
        name="finish",
    )(acc, lg, rg, basis3, left, right, basis3, basis4)


def fast(rows, cols, left, right, basis, block):
    acc, lg, rg = gather_product(left, right, basis, block, rows, cols)
    return finish(acc, lg, rg, left, right, basis, rows, cols)


def plain(left, right, basis, block):
    ml = left.shape[0]
    mr = right.shape[0]
    whole_left = lax.all_gather(left, "col", axis=0, tiled=True)
    whole_right = lax.all_gather(right, "row", axis=0, tiled=True)
    bl = lax.dynamic_slice_in_dim(basis, lax.axis_index("col") * ml, ml, 0)
    br = lax.dynamic_slice_in_dim(basis, lax.axis_index("row") * mr, mr, 0)
    lc = dot(basis, whole_left, ((0,), (0,)))
    rc = dot(basis, whole_right, ((0,), (0,)))
    updated = block + dot(whole_left, whole_right, ((0,), (0,))) - dot(lc, rc, ((0,), (0,)))
    left_reduced = left - dot(bl, lc, ((1,), (0,)))
    right_reduced = right - dot(br, rc, ((1,), (0,)))
    return updated, left_reduced, right_reduced


def solution(mesh):
    rows, cols = mesh.shape["row"], mesh.shape["col"]
    local = functools.partial(fast, rows, cols) if (rows, cols) == (4, 8) else plain
    in_specs = (P("col", "row"), P("row", "col"), P(), P("row", "col"))
    out_specs = (P("row", "col"), P("col", "row"), P("row", "col"))
    return jax.shard_map(
        local, mesh=mesh, in_specs=in_specs, out_specs=out_specs, check_vma=False
    )
```
